128 devices in a mesh: lo: 16 (over z, y), hi: 8 (over x, core).
Axes of the slice: x: 4, y: 4, z: 4, core: 2. Of those that a mesh axis runs over, the one named last changes fastest.
Arguments:
- contribution: float32 [8, 16, 1024, 1024], P('hi', 'lo'), as said below
- pivot_one: float32 [8, 16, 384, 768], P('hi', 'lo'), as said below
- rows_one: float32 [8, 16, 768, 2304], P('hi', 'lo'), as said below
- pivot_two: float32 [8, 16, 192, 768], P('hi', 'lo'), as said below
- rows_two: float32 [8, 16, 384, 2304], P('hi', 'lo'), as said below
- map_one: int32 [8, 16, 8], replicated, may hold values from 0 to 17, as said below
- map_two: int32 [8, 8, 12], replicated, may hold values from 0 to 17, as said below
- fill_one: int32 [8, 8, 12, 6], replicated, may hold values 0 or 1
- fill_two: int32 [4, 8, 12, 6], replicated, may hold values 0 or 1
- live_one: int32 [8, 8], replicated, may hold values from 3 to 6, as said below
- live_two: int32 [4, 8], replicated, may hold values from 3 to 6, as said below
Outputs:
- lower_one: float32 [8, 16, 384, 768], P('hi', 'lo')
- panel_one: float32 [8, 16, 768, 768], P('hi', 'lo')
- lower_two: float32 [8, 16, 192, 768], P('hi', 'lo')
- panel_two: float32 [8, 16, 384, 768], P('hi', 'lo')
- schur_two: float32 [8, 16, 384, 1536], P('hi', 'lo')
The draws below stay inside these ranges and needn't reach their ends.
Inputs may be any that keep to these rules, and one draw needn't show every extreme that they name: `contribution`: symmetric and negative semidefinite: minus a Gram matrix, divided by 1024. `pivot_one`: with rows_one, the rows of a symmetric matrix of each front with a dominant diagonal. `rows_one`: with pivot_one, the rows of a symmetric matrix of each front with a dominant diagonal. `pivot_two`: with rows_two, the rows of a symmetric matrix of each front with a dominant diagonal. `rows_two`: with pivot_two, the rows of a symmetric matrix of each front with a dominant diagonal. `map_one`: each device's list names 8 distinct tiles. `map_two`: each front's list names 12 distinct tiles. `live_one`: both ends reached in every draw. `live_two`: both ends reached in every draw.
All inputs are finite; a program needn't handle non-finite values.
Results may differ from the reference program's by a relative error of at most 0.0003.
Values sent between devices are 32-bit elements; how exact they have to be, the bound alone decides.
A program may use at most 192 MiB of HBM per device.

```python
import math
import jax
import jax.numpy as jnp
from jax import lax

TILE = 128
CT = 8
P1T = 6
U1T = 12
P2T = 6
U2T = 12
N_LO = 16
N_HI = 8


def base_normal(key, shape):
    return jax.random.normal(key, shape, jnp.float32)


def front_blocks(key, tag, count_hi, count_lo, pivot_size, rest_size):
    sub_keys = jax.random.split(jax.random.fold_in(key, tag), 3)
    entry_scale = 1.0 / math.sqrt(pivot_size + rest_size)
    upper_part = base_normal(sub_keys[0], (count_hi, count_lo, pivot_size, pivot_size))
    pivot_part = (upper_part + jnp.swapaxes(upper_part, -1, -2)) * (entry_scale / math.sqrt(2.0)) + 12.0 * jnp.eye(pivot_size, dtype=jnp.float32)
    coupling = base_normal(sub_keys[1], (count_hi, count_lo, rest_size, pivot_size)) * entry_scale
    trailing_part = base_normal(sub_keys[2], (count_hi, count_lo, rest_size, rest_size))
    trailing_part = (trailing_part + jnp.swapaxes(trailing_part, -1, -2)) * (entry_scale / math.sqrt(2.0)) + 12.0 * jnp.eye(rest_size, dtype=jnp.float32)
    return (pivot_part, jnp.concatenate([coupling, trailing_part], axis=-1))


def split_one(fronts):
    row_count = fronts.shape[2]
    grouped = fronts.reshape(N_HI, N_LO // 2, 2, row_count // 2, fronts.shape[3])
    return grouped.transpose(0, 2, 1, 3, 4).reshape(N_HI, N_LO, row_count // 2, fronts.shape[3])


def split_two(fronts):
    row_count = fronts.shape[2]
    grouped = fronts.reshape(N_HI // 2, N_LO // 2, 2, 2, row_count // 4, fronts.shape[3])
    return grouped.transpose(2, 0, 3, 1, 4, 5).reshape(N_HI, N_LO, row_count // 4, fronts.shape[3])


def draw_contribution(key, part):
    order_size = CT * TILE
    factor_part = base_normal(jax.random.fold_in(key, 11), (N_HI, N_LO, order_size, order_size))
    return -jnp.einsum('hlik,hljk->hlij', factor_part, factor_part) / order_size


def draw_pivot_one(key, part):
    pivot_part, rows_part = front_blocks(key, 21, N_HI, N_LO // 2, P1T * TILE, U1T * TILE)
    return split_one(pivot_part)


def draw_rows_one(key, part):
    pivot_part, rows_part = front_blocks(key, 21, N_HI, N_LO // 2, P1T * TILE, U1T * TILE)
    return split_one(rows_part)


def draw_pivot_two(key, part):
    pivot_part, rows_part = front_blocks(key, 22, N_HI // 2, N_LO // 2, P2T * TILE, U2T * TILE)
    return split_two(pivot_part)


def draw_rows_two(key, part):
    pivot_part, rows_part = front_blocks(key, 22, N_HI // 2, N_LO // 2, P2T * TILE, U2T * TILE)
    return split_two(rows_part)


def draw_map_one(key, part):
    sub_keys = jax.random.split(jax.random.fold_in(key, 31), N_HI * N_LO)
    chosen = jax.vmap(lambda single: jax.random.permutation(single, P1T + U1T)[:CT])(sub_keys)
    return chosen.reshape(N_HI, N_LO, CT).astype(jnp.int32)


def draw_map_two(key, part):
    sub_keys = jax.random.split(jax.random.fold_in(key, 32), N_HI * (N_LO // 2))
    chosen = jax.vmap(lambda single: jax.random.permutation(single, P2T + U2T)[:U1T])(sub_keys)
    return chosen.reshape(N_HI, N_LO // 2, U1T).astype(jnp.int32)


def draw_live_one(key, part):
    counts = jax.random.randint(jax.random.fold_in(key, 41), (N_HI, N_LO // 2), P1T // 2, P1T + 1)
    counts = counts.at[0, 0].set(P1T).at[0, 1].set(P1T // 2)
    return counts.astype(jnp.int32)


def draw_live_two(key, part):
    counts = jax.random.randint(jax.random.fold_in(key, 42), (N_HI // 2, N_LO // 2), P2T // 2, P2T + 1)
    counts = counts.at[0, 0].set(P2T).at[0, 1].set(P2T // 2)
    return counts.astype(jnp.int32)


def plant(array, own_key, smallest, top_value):
    longest = array.shape.index(max(array.shape))
    spots = []
    for shift in (0, 1):
        where = [jax.random.randint(jax.random.fold_in(own_key, axis), (), 0, length) for axis, length in enumerate(array.shape)]
        where[longest] = (where[longest] + shift) % array.shape[longest]
        spots.append(tuple(where))
    return array.at[spots[0]].set(smallest).at[spots[1]].set(top_value)


def setup_inputs(seed: int = 0) -> dict:
    key_of = jax.random.split(jax.random.key(seed), 12)
    contribution = draw_contribution(jax.random.fold_in(key_of[11], 71), 0)
    pivot_one = draw_pivot_one(jax.random.fold_in(key_of[11], 71), 0)
    rows_one = draw_rows_one(jax.random.fold_in(key_of[11], 71), 0)
    pivot_two = draw_pivot_two(jax.random.fold_in(key_of[11], 71), 0)
    rows_two = draw_rows_two(jax.random.fold_in(key_of[11], 71), 0)
    map_one = draw_map_one(jax.random.fold_in(key_of[11], 71), 0)
    map_two = draw_map_two(jax.random.fold_in(key_of[11], 71), 0)
    fill_one = plant((jax.random.randint(key_of[7], (N_HI, N_LO // 2, U1T, P1T), 0, 3) < 2).astype(jnp.int32), jax.random.fold_in(key_of[7], 1), 0, 1)
    fill_two = plant((jax.random.randint(key_of[8], (N_HI // 2, N_LO // 2, U2T, P2T), 0, 3) < 2).astype(jnp.int32), jax.random.fold_in(key_of[8], 1), 0, 1)
    live_one = draw_live_one(jax.random.fold_in(key_of[11], 71), 0)
    live_two = draw_live_two(jax.random.fold_in(key_of[11], 71), 0)
    return {"contribution": contribution, "pivot_one": pivot_one, "rows_one": rows_one, "pivot_two": pivot_two, "rows_two": rows_two, "map_one": map_one, "map_two": map_two, "fill_one": fill_one, "fill_two": fill_two, "live_one": live_one, "live_two": live_two}


HIGHEST_MODE = lax.Precision.HIGHEST

def spread(source_block, row_map, col_map, row_first, row_tiles, col_tiles):
    row_count = row_map.shape[0]
    col_count = col_map.shape[0]
    tile_size = source_block.shape[1] // col_count
    targets = row_first + jnp.arange(row_tiles, dtype=jnp.int32)
    row_onehot = (row_map[:, None] == targets[None, :]).astype(jnp.float32)
    col_onehot = (col_map[:, None] == jnp.arange(col_tiles, dtype=jnp.int32)[None, :]).astype(jnp.float32)
    blocks = source_block.reshape(row_count, tile_size, col_count, tile_size)
    placed = jnp.einsum('ia,ixky->axky', row_onehot, blocks, precision=HIGHEST_MODE)
    placed = jnp.einsum('axky,kb->axby', placed, col_onehot, precision=HIGHEST_MODE)
    return placed.reshape(row_tiles * tile_size, col_tiles * tile_size)

def factor(pivot_block, coupling, live_tiles):
    kept = (jnp.arange(pivot_block.shape[0]) // TILE < live_tiles).astype(pivot_block.dtype)
    pivot_block = pivot_block * kept[:, None] * kept[None, :] + jnp.diag(1.0 - kept)
    coupling = coupling * kept[None, :]
    factor_lower = jnp.linalg.cholesky(pivot_block)
    panel_part = lax.linalg.triangular_solve(factor_lower, coupling, left_side=False, lower=True, transpose_a=True)
    return (factor_lower, panel_part)

def expand_fill(fill_tiles):
    return jnp.repeat(jnp.repeat(fill_tiles, TILE, axis=0), TILE, axis=1).astype(jnp.float32)

def to_fronts(values_in):
    grouped = values_in.reshape((2, N_HI // 2, 2, N_LO // 2) + values_in.shape[2:])
    axes_order = (1, 3, 0, 2) + tuple(range(4, grouped.ndim))
    return grouped.transpose(axes_order)

def table_fronts(table_in):
    grouped = table_in.reshape((2, N_HI // 2) + table_in.shape[1:])
    return jnp.moveaxis(grouped, 0, 2)

def to_devices(stacked):
    grouped = stacked.reshape((N_HI // 2, N_LO // 2) + stacked.shape[1:])
    axes_order = (2, 0, 3, 1) + tuple(range(4, grouped.ndim))
    return grouped.transpose(axes_order).reshape((N_HI, N_LO) + grouped.shape[4:])

def one_quad(quad_items):
    blocks, maps_first, maps_second, pivots_first, rows_first, fills_first, lives_first, pivots_second, rows_second, fill_second, live_second = quad_items
    pivot_size = P1T * TILE
    rest_size = U1T * TILE
    second_size = P2T * TILE
    second_rest = U2T * TILE
    lowers = []
    panels = []
    schurs = []
    for which_side in range(2):
        pivot_block = pivots_first[which_side].reshape(pivot_size, pivot_size)
        front_rows = rows_first[which_side].reshape(rest_size, pivot_size + rest_size)
        coupling = front_rows[:, :pivot_size] * expand_fill(fills_first[which_side])
        trailing = front_rows[:, pivot_size:]
        for which_half in range(2):
            child_block = blocks[which_side, which_half]
            child_map = maps_first[which_side, which_half]
            pivot_block = pivot_block + spread(child_block, child_map, child_map, 0, P1T, P1T)
            placed_rows = spread(child_block, child_map, child_map, P1T, U1T, P1T + U1T)
            coupling = coupling + placed_rows[:, :pivot_size]
            trailing = trailing + placed_rows[:, pivot_size:]
        factor_lower, panel_part = factor(pivot_block, coupling, lives_first[which_side])
        schurs.append(trailing - jnp.dot(panel_part, panel_part.T, precision=HIGHEST_MODE))
        lowers.append(factor_lower.reshape(2, pivot_size // 2, pivot_size))
        panels.append(panel_part.reshape(2, rest_size // 2, pivot_size))
    pivot_block = pivots_second.reshape(second_size, second_size)
    front_rows = rows_second.reshape(second_rest, second_size + second_rest)
    coupling = front_rows[:, :second_size] * expand_fill(fill_second)
    trailing = front_rows[:, second_size:]
    for which_side in range(2):
        child_map = maps_second[which_side]
        pivot_block = pivot_block + spread(schurs[which_side], child_map, child_map, 0, P2T, P2T)
        placed_rows = spread(schurs[which_side], child_map, child_map, P2T, U2T, P2T + U2T)
        coupling = coupling + placed_rows[:, :second_size]
        trailing = trailing + placed_rows[:, second_size:]
    lower_full, panel_full = factor(pivot_block, coupling, live_second)
    schur_full = trailing - jnp.dot(panel_full, panel_full.T, precision=HIGHEST_MODE)
    return (jnp.stack(lowers), jnp.stack(panels), lower_full.reshape(2, 2, second_size // 4, second_size), panel_full.reshape(2, 2, second_rest // 4, second_size), schur_full.reshape(2, 2, second_rest // 4, second_rest))

def reference(contribution, pivot_one, rows_one, pivot_two, rows_two, map_one, map_two, fill_one, fill_two, live_one, live_two):
    quad_items = (to_fronts(contribution), to_fronts(map_one), table_fronts(map_two), to_fronts(pivot_one), to_fronts(rows_one), table_fronts(fill_one), table_fronts(live_one), to_fronts(pivot_two), to_fronts(rows_two), fill_two, live_two)
    flat_items = jax.tree.map(lambda member: member.reshape((-1,) + member.shape[2:]), quad_items)
    quad_results = lax.map(one_quad, flat_items)
    lower_first, panel_first, lower_second, panel_second, schur_second = quad_results
    return (to_devices(lower_first), to_devices(panel_first), to_devices(lower_second), to_devices(panel_second), to_devices(schur_second))
```

```python
import jax
import jax.numpy as jnp
from jax import lax
from jax.experimental import pallas as pl
from jax.experimental.pallas import tpu as pltpu
from jax.sharding import PartitionSpec as P

TILE = 128
P1T = 6
U1T = 12
P2T = 6
U2T = 12


HIGHEST_MODE = lax.Precision.HIGHEST


def partner(array, axis, apart):
    return lax.ppermute(array, axis, [(i, i ^ 1 << apart) for i in range(lax.axis_size(axis))])


def spread(source_block, row_map, col_map, row_first, row_tiles, col_tiles):
    row_count = row_map.shape[0]
    col_count = col_map.shape[0]
    tile_size = source_block.shape[1] // col_count
    targets = row_first + jnp.arange(row_tiles, dtype=jnp.int32)
    row_onehot = (row_map[:, None] == targets[None, :]).astype(jnp.float32)
    col_onehot = (col_map[:, None] == jnp.arange(col_tiles, dtype=jnp.int32)[None, :]).astype(
        jnp.float32
    )
    blocks = source_block.reshape(row_count, tile_size, col_count, tile_size)
    placed = jnp.einsum("ia,ixky->axky", row_onehot, blocks, precision=HIGHEST_MODE)
    placed = jnp.einsum("axky,kb->axby", placed, col_onehot, precision=HIGHEST_MODE)
    return placed.reshape(row_tiles * tile_size, col_tiles * tile_size)


T=128
f32 = jnp.float32
bf16=jnp.bfloat16

def split(x):
    hi=x.astype(bf16)
    return hi,(x-hi.astype(f32)).astype(bf16)

def dot3(a,b,dims):
    ah,al=a; bh,bl=b
    dn=(dims,((),()))
    f=lambda x,y: lax.dot_general(x,y,dn,preferred_element_type=f32)
    return f(ah,bh)+(f(ah,bl)+f(al,bh))

NN=((1,),(0,)); NT=((1,),(1,)); TN=((0,),(0,))

def factor_tile(d_ref,w_ref,u_ref):
    lane=lax.broadcasted_iota(jnp.int32,(8,T),1)
    for g in range(16):
        r0=8*g
        sub=lax.broadcasted_iota(jnp.int32,(8,T),0)+r0
        w_ref[r0:r0+8,:]=jnp.where(lane==sub,1.0,0.0).astype(f32)
    for g in range(16):
        r0=8*g
        rows=[jnp.broadcast_to(d_ref[r0+i:r0+i+1,:],(8,T)) for i in range(8)]
        wrows=[jnp.broadcast_to(w_ref[r0+i:r0+i+1,:],(8,T)) for i in range(8)]
        E=[[jnp.broadcast_to(rows[i][:,r0+k:r0+k+1],(8,T)) for k in range(i+1)] for i in range(8)]
        l=[[None]*8 for _ in range(8)]
        rinv=[None]*8
        for j in range(8):
            rinv[j]=lax.rsqrt(E[j][j])
            for i in range(j+1,8):
                l[i][j]=E[i][j]*rinv[j]
            for i in range(j+1,8):
                for k in range(j+1,i+1):
                    E[i][k]=E[i][k]-l[i][j]*l[k][j]
        u=[None]*8; w=[None]*8
        for j in range(8):
            a=rows[j]; b=wrows[j]
            for k in range(j):
                a=a-l[j][k]*u[k]
                b=b-l[j][k]*w[k]
            u[j]=a*rinv[j]; w[j]=b*rinv[j]
            u_ref[r0+j:r0+j+1,:]=jnp.where(lane[:1]>=r0+j,u[j][:1],0.0)
            w_ref[r0+j:r0+j+1,:]=w[j][:1]
        for r in range(g+1,16):
            q=8*r
            dr=d_ref[q:q+8,:]; wr=w_ref[q:q+8,:]
            c=[jnp.broadcast_to(dr[:,r0+k:r0+k+1],(8,T)) for k in range(8)]
            for j in range(8):
                a=c[j]
                for k in range(j):
                    a=a-l[j][k]*c[k]
                c[j]=a*rinv[j]
            for j in range(8):
                dr=dr-c[j]*u[j]
                wr=wr-c[j]*w[j]
            d_ref[q:q+8,:]=dr
            w_ref[q:q+8,:]=wr

def factor_kernel(live_ref,a_ref,c_ref,l_ref,p_ref,a_s,d_s,w_s,u_s,lk_h,lk_l):
    n=a_ref.shape[0]//T
    m=c_ref.shape[0]
    live=live_ref[0]
    l_ref[...]=jnp.zeros_like(l_ref)
    p_ref[...]=jnp.zeros_like(p_ref)
    a_s[...]=a_ref[...]
    ii=lax.broadcasted_iota(jnp.int32,(T,T),0); jj=lax.broadcasted_iota(jnp.int32,(T,T),1)
    eye=jnp.where(ii==jj,1.0,0.0).astype(f32)
    def dead(k,_):
        s=pl.ds(pl.multiple_of(k*T,T),T)
        l_ref[s,s]=eye
        return 0
    lax.fori_loop(live,n,dead,0)
    def cp(k,_):
        s=pl.ds(pl.multiple_of(k*T,T),T)
        p_ref[:,s]=c_ref[:,s]
        return 0
    lax.fori_loop(0,live,cp,0)
    def step(k,_):
        s=pl.ds(pl.multiple_of(k*T,T),T)
        d_s[...]=a_s[s,s]
        factor_tile(d_s,w_s,u_s)
        l_ref[s,s]=u_s[...].T
        w=split(w_s[...])
        pk=dot3(split(p_ref[:,s]),w,NT)
        p_ref[:,s]=pk
        pks=split(pk)
        def panel(i,_):
            si=pl.ds(pl.multiple_of(i*T,T),T)
            x=dot3(split(a_s[si,s]),w,NT)
            l_ref[si,s]=x
            xh,xl=split(x)
            lk_h[si,:]=xh; lk_l[si,:]=xl
            p_ref[:,si]=p_ref[:,si]-dot3(pks,(xh,xl),NT)
            return 0
        lax.fori_loop(k+1,live,panel,0)
        def upd(j,_):
            sj=pl.ds(pl.multiple_of(j*T,T),T)
            xj=(lk_h[sj,:],lk_l[sj,:])
            def upd2(i,_):
                si=pl.ds(pl.multiple_of(i*T,T),T)
                a_s[si,sj]=a_s[si,sj]-dot3((lk_h[si,:],lk_l[si,:]),xj,NT)
                return 0
            lax.fori_loop(j,live,upd2,0)
            return 0
        lax.fori_loop(k+1,live,upd,0)
        return 0
    lax.fori_loop(0,live,step,0)

def factor(pivot,coupling,live):
    n=pivot.shape[0]; m=coupling.shape[0]
    return pl.pallas_call(factor_kernel,
        grid_spec=pltpu.PrefetchScalarGridSpec(num_scalar_prefetch=1,grid=(),
            in_specs=[pl.BlockSpec(memory_space=pltpu.VMEM)]*2,
            out_specs=[pl.BlockSpec(memory_space=pltpu.VMEM)]*2,
            scratch_shapes=[pltpu.VMEM((n,n),f32),pltpu.VMEM((T,T),f32),pltpu.VMEM((T,T),f32),pltpu.VMEM((T,T),f32),pltpu.VMEM((n,T),bf16),pltpu.VMEM((n,T),bf16)]),
        out_shape=[jax.ShapeDtypeStruct((n,n),f32),jax.ShapeDtypeStruct((m,n),f32)],
        name="factor")(live.reshape(1),pivot,coupling)


def expand_fill(fill_tiles):
    return jnp.repeat(jnp.repeat(fill_tiles, TILE, axis=0), TILE, axis=1).astype(jnp.float32)


def across_lo(values_in):
    return partner(values_in, "lo", lax.axis_size("lo").bit_length() - 2)


def across_hi(values_in):
    return partner(values_in, "hi", lax.axis_size("hi").bit_length() - 2)


def ordered(mine, theirs, which_side):
    first_half = jnp.where(which_side == 0, mine, theirs)
    second_half = jnp.where(which_side == 0, theirs, mine)
    return jnp.concatenate([first_half, second_half], axis=0)


def body(
    contribution,
    pivot_one,
    rows_one,
    pivot_two,
    rows_two,
    map_one,
    map_two,
    fill_one,
    fill_two,
    live_one,
    live_two,
):
    size_lo = lax.axis_size("lo")
    size_hi = lax.axis_size("hi")
    half_lo = size_lo // 2
    half_hi = size_hi // 2
    index_lo = lax.axis_index("lo")
    index_hi = lax.axis_index("hi")
    side_lo = index_lo // half_lo
    side_hi = index_hi // half_hi
    front_lo = index_lo % half_lo
    front_hi = index_hi % half_hi
    pivot_size = P1T * TILE
    half_tiles = U1T // 2
    own_block = contribution[0, 0]
    own_map = map_one[index_hi, index_lo]
    own_pivot = pivot_one[0, 0]
    fill_tiles = lax.dynamic_slice_in_dim(
        fill_one[index_hi, front_lo], side_lo * half_tiles, half_tiles, 0
    )
    own_rows = rows_one[0, 0]
    own_rows = jnp.concatenate(
        [own_rows[:, :pivot_size] * expand_fill(fill_tiles), own_rows[:, pivot_size:]], axis=1
    )
    own_start = P1T + side_lo * half_tiles
    placed_pivot = lax.dynamic_update_slice(
        jnp.zeros((pivot_size, pivot_size), jnp.float32),
        own_pivot,
        (side_lo * (pivot_size // 2), 0),
    )
    other_block, other_pivot = partner((own_block, own_pivot), "lo", size_lo.bit_length() - 2)
    other_map = map_one[index_hi, (index_lo + half_lo) % size_lo]
    placed_pivot = lax.dynamic_update_slice(
        placed_pivot, other_pivot, ((1 - side_lo) * (pivot_size // 2), 0)
    )
    pivot_block = (
        placed_pivot
        + spread(own_block, own_map, own_map, 0, P1T, P1T)
        + spread(other_block, other_map, other_map, 0, P1T, P1T)
    )
    front_rows = (
        own_rows
        + spread(own_block, own_map, own_map, own_start, half_tiles, P1T + U1T)
        + spread(other_block, other_map, other_map, own_start, half_tiles, P1T + U1T)
    )
    factor_lower, panel_part = factor(
        pivot_block, front_rows[:, :pivot_size], live_one[index_hi, front_lo]
    )
    full_panel = ordered(panel_part, across_lo(panel_part), side_lo)
    schur_rows = front_rows[:, pivot_size:] - jnp.dot(
        panel_part, full_panel.T, precision=HIGHEST_MODE
    )
    lower_one = lax.dynamic_slice_in_dim(
        factor_lower, side_lo * (pivot_size // 2), pivot_size // 2, 0
    )
    second_size = P2T * TILE
    quarter_tiles = U2T // 4
    quarter_rows = quarter_tiles * TILE
    quarter_pivot = second_size // 4
    second_width = (P2T + U2T) * TILE
    quarter = 2 * side_hi + side_lo
    second_map = map_two[index_hi, front_lo]
    row_map = lax.dynamic_slice_in_dim(second_map, side_lo * half_tiles, half_tiles, 0)
    pivot_part = lax.dynamic_update_slice(
        jnp.zeros((second_size, second_size), jnp.float32),
        pivot_two[0, 0],
        (quarter * quarter_pivot, 0),
    )
    pivot_part = pivot_part + spread(schur_rows, row_map, second_map, 0, P2T, P2T)
    part_rows = spread(schur_rows, row_map, second_map, P2T, U2T, P2T + U2T)
    grouped = part_rows.reshape(2, 2 * quarter_rows, second_width)
    got_pivot, got_rows = across_hi((pivot_part, grouped[1 - side_hi]))
    pivot_part = pivot_part + got_pivot
    kept_rows = (grouped[side_hi] + got_rows).reshape(2, quarter_rows, second_width)
    got_pivot, got_rows = across_lo((pivot_part, kept_rows[1 - side_lo]))
    second_pivot = pivot_part + got_pivot
    quarter_part = kept_rows[side_lo] + got_rows
    fill_second = lax.dynamic_slice_in_dim(
        fill_two[front_hi, front_lo], quarter * quarter_tiles, quarter_tiles, 0
    )
    own_second = rows_two[0, 0]
    quarter_part = quarter_part + jnp.concatenate(
        [own_second[:, :second_size] * expand_fill(fill_second), own_second[:, second_size:]],
        axis=1,
    )
    lower_full, panel_two = factor(
        second_pivot, quarter_part[:, :second_size], live_two[front_hi, front_lo]
    )
    pair_panel = ordered(panel_two, across_lo(panel_two), side_lo)
    all_panel = ordered(pair_panel, across_hi(pair_panel), side_hi)
    schur_two = quarter_part[:, second_size:] - jnp.dot(
        panel_two, all_panel.T, precision=HIGHEST_MODE
    )
    lower_two = lax.dynamic_slice_in_dim(lower_full, quarter * quarter_pivot, quarter_pivot, 0)
    return (
        lower_one[None, None],
        panel_part[None, None],
        lower_two[None, None],
        panel_two[None, None],
        schur_two[None, None],
    )


def solution(mesh):
    placed = (
        P("hi", "lo", None, None),
        P("hi", "lo", None, None),
        P("hi", "lo", None, None),
        P("hi", "lo", None, None),
        P("hi", "lo", None, None),
        P(),
        P(),
        P(),
        P(),
        P(),
        P(),
    )
    return jax.shard_map(
        body,
        mesh=mesh,
        in_specs=placed,
        out_specs=(
            P("hi", "lo", None, None),
            P("hi", "lo", None, None),
            P("hi", "lo", None, None),
            P("hi", "lo", None, None),
            P("hi", "lo", None, None),
        ),
        check_vma=False,
    )
```

```python
import functools
import jax
import jax.numpy as jnp
from jax import lax
from jax.experimental import pallas as pl
from jax.experimental.pallas import tpu as pltpu
from jax.sharding import PartitionSpec as P

T = 128
NP = 6
NU = 12
NC = 8
f32 = jnp.float32
bf16 = jnp.bfloat16
NN = ((1,), (0,))
NT = ((1,), (1,))
OWN, OTH, MAP2, SLO, SHI, LIVE1, LIVE2, FILL1, FILL2 = 0, 8, 16, 28, 29, 30, 31, 32, 68


def tl(i):
    return pl.ds(pl.multiple_of(i * T, T), T)


def split(x):
    hi = x.astype(bf16)
    return hi, (x - hi.astype(f32)).astype(bf16)


def dot3(a, b, dims):
    (ah, al), (bh, bl) = a, b
    dn = (dims, ((), ()))
    f = lambda x, y: lax.dot_general(x, y, dn, preferred_element_type=f32)
    return f(ah, bh) + (f(ah, bl) + f(al, bh))


def call(kernel, args, specs, outs, scratch, name, flops=0, grid=(1,)):
    whole = pl.BlockSpec(memory_space=pltpu.VMEM)
    in_specs = [whole if s is None else s for s in specs]
    nbytes = sum(4 * a.size for a in args[1:]) + sum(4 * o.size for o in outs)
    return pl.pallas_call(
        kernel,
        grid_spec=pltpu.PrefetchScalarGridSpec(
            num_scalar_prefetch=1,
            grid=grid,
            in_specs=in_specs,
            out_specs=[whole] * len(outs),
            scratch_shapes=scratch,
        ),
        out_shape=outs,
        compiler_params=pltpu.CompilerParams(vmem_limit_bytes=60 * 1024 * 1024),
        cost_estimate=pl.CostEstimate(flops=flops, bytes_accessed=nbytes, transcendentals=0),
        name=name,
    )(*args)


def shape(*dims, dtype=f32):
    return jax.ShapeDtypeStruct(dims, dtype)


def block(rows, cols, j):
    return pl.BlockSpec((rows, cols), lambda i, s: (0, j))


def invert(s_ref, first, count, inv_ref, size):
    for r in range(size):
        inv_ref[r] = -1
    for i in range(count):
        inv_ref[s_ref[first + i]] = i


def gather_one_kernel(s_ref, c_ref, p_ref, piv_ref, coup_ref, inv):
    side = s_ref[SLO]
    invert(s_ref, OWN, NC, inv, 18)

    def piv_row(r, _):
        local = r - 3 * side

        def piv_col(c, _):
            at = r * (r + 1) // 2 + c

            @pl.when((local >= 0) & (local < 3))
            def _():
                piv_ref[at] = p_ref[tl(local), tl(c)]

            @pl.when((local < 0) | (local >= 3))
            def _():
                piv_ref[at] = jnp.zeros((T, T), f32)

            @pl.when((inv[r] >= 0) & (inv[c] >= 0))
            def _():
                piv_ref[at] += c_ref[tl(inv[r]), tl(inv[c])]

            return 0

        return lax.fori_loop(0, r + 1, piv_col, 0)

    lax.fori_loop(0, NP, piv_row, 0)

    def coup_tile(t, count):
        row = inv[NP + (1 - side) * 6 + t // NP]
        col = inv[t % NP]
        hit = (row >= 0) & (col >= 0)

        @pl.when(hit)
        def _():
            coup_ref[count] = c_ref[tl(row), tl(col)]

        return count + hit.astype(jnp.int32)

    lax.fori_loop(0, 36, coup_tile, 0)


def factor_tile(d_ref, w_ref, u_ref):
    lane = lax.broadcasted_iota(jnp.int32, (8, T), 1)
    row = lax.broadcasted_iota(jnp.int32, (8, T), 0)
    for g in range(16):
        r0 = 8 * g
        w_ref[r0 : r0 + 8, :] = jnp.where(lane == row + r0, 1.0, 0.0).astype(f32)
    for g in range(16):
        r0 = 8 * g
        rows = [jnp.broadcast_to(d_ref[r0 + i : r0 + i + 1, :], (8, T)) for i in range(8)]
        wrows = [jnp.broadcast_to(w_ref[r0 + i : r0 + i + 1, :], (8, T)) for i in range(8)]
        e = [
            [jnp.broadcast_to(rows[i][:, r0 + k : r0 + k + 1], (8, T)) for k in range(i + 1)]
            for i in range(8)
        ]
        l = [[None] * 8 for _ in range(8)]
        rinv = [None] * 8
        for j in range(8):
            rinv[j] = lax.rsqrt(e[j][j])
            for i in range(j + 1, 8):
                l[i][j] = e[i][j] * rinv[j]
            for i in range(j + 1, 8):
                for k in range(j + 1, i + 1):
                    e[i][k] = e[i][k] - l[i][j] * l[k][j]
        u = [None] * 8
        w = [None] * 8
        for j in range(8):
            a = rows[j]
            b = wrows[j]
            for k in range(j):
                a = a - l[j][k] * u[k]
                b = b - l[j][k] * w[k]
            u[j] = a * rinv[j]
            w[j] = b * rinv[j]
            u_ref[r0 + j : r0 + j + 1, :] = jnp.where(lane[:1] >= r0 + j, u[j][:1], 0.0)
            w_ref[r0 + j : r0 + j + 1, :] = w[j][:1]
        for r in range(g + 1, 16):
            q = 8 * r
            dr = d_ref[q : q + 8, :]
            wr = w_ref[q : q + 8, :]
            c = [jnp.broadcast_to(dr[:, r0 + k : r0 + k + 1], (8, T)) for k in range(8)]
            for j in range(8):
                a = c[j]
                for k in range(j):
                    a = a - l[j][k] * c[k]
                c[j] = a * rinv[j]
            for j in range(8):
                dr = dr - c[j] * u[j]
                wr = wr - c[j] * w[j]
            d_ref[q : q + 8, :] = dr
            w_ref[q : q + 8, :] = wr


def factor_kernel(counts, live_at, take, s_ref, *refs):
    n_in = 2 * len(counts)
    ins = refs[:n_in]
    low_ref, lh_ref, ll_ref, wh_ref, wl_ref, a_s, l_s, d_s, w_s, u_s = refs[n_in:]
    live = s_ref[live_at]
    first = 0
    spots = [(r, c) for r in range(NP) for c in range(r + 1)]
    for n, count in enumerate(counts):
        for t in range(count):
            r, c = spots[first + t]
            a_s[r * T : r * T + T, c * T : c * T + T] = ins[2 * n][t] + ins[2 * n + 1][t]
        first += count
    l_s[...] = jnp.zeros_like(l_s)
    ii = lax.broadcasted_iota(jnp.int32, (T, T), 0)
    jj = lax.broadcasted_iota(jnp.int32, (T, T), 1)
    eye = jnp.where(ii == jj, 1.0, 0.0).astype(f32)

    def dead(k, _):
        l_s[tl(k), tl(k)] = eye
        return 0

    lax.fori_loop(live, NP, dead, 0)

    def step(k, _):
        s = tl(k)
        d_s[...] = a_s[s, s]
        factor_tile(d_s, w_s, u_s)
        l_s[s, s] = u_s[...].T
        w = split(w_s[...])
        wh_ref[s, :] = w[0]
        wl_ref[s, :] = w[1]

        def panel(i, _):
            x = dot3(split(a_s[tl(i), s]), w, NT)
            l_s[tl(i), s] = x
            xh, xl = split(x)
            lh_ref[tl(i), s] = xh
            ll_ref[tl(i), s] = xl
            return 0

        lax.fori_loop(k + 1, live, panel, 0)

        def col(j, _):
            xj = (lh_ref[tl(j), s], ll_ref[tl(j), s])

            def tile(i, _):
                xi = (lh_ref[tl(i), s], ll_ref[tl(i), s])
                a_s[tl(i), tl(j)] = a_s[tl(i), tl(j)] - dot3(xi, xj, NT)
                return 0

            return lax.fori_loop(j, live, tile, 0)

        return lax.fori_loop(k + 1, live, col, 0)

    lax.fori_loop(0, live, step, 0)
    low_ref[...] = l_s[pl.ds(pl.multiple_of(take(s_ref), 64), low_ref.shape[0]), :]


def factor(scalars, pairs, live_at, take, rows, name):
    counts = tuple(x.shape[0] for x, _ in pairs)
    n = NP * T
    return call(
        functools.partial(factor_kernel, counts, live_at, take),
        [scalars] + [x for pair in pairs for x in pair],
        [None] * (2 * len(pairs)),
        [shape(rows, n), shape(n, n, dtype=bf16), shape(n, n, dtype=bf16)]
        + [shape(n, T, dtype=bf16)] * 2,
        [pltpu.VMEM((n, n), f32)] * 2 + [pltpu.VMEM((T, T), f32)] * 3,
        name,
        flops=20_000_000_000,
    )


def solve(x_ref, live, lh_ref, ll_ref, wh_ref, wl_ref, ph, plo):
    for k in range(NP):
        s = slice(k * T, k * T + T)

        @pl.when(k < live)
        def _():
            x = x_ref[:, s]
            if k:
                b = slice(0, k * T)
                x = x - dot3((ph[:, b], plo[:, b]), (lh_ref[s, b], ll_ref[s, b]), NT)
            x = dot3(split(x), (wh_ref[s, :], wl_ref[s, :]), NT)
            x_ref[:, s] = x
            xh, xl = split(x)
            ph[:, s] = xh
            plo[:, s] = xl

        @pl.when(k >= live)
        def _():
            x_ref[:, s] = jnp.zeros_like(x_ref[:, s])
            ph[:, s] = jnp.zeros_like(ph[:, s])
            plo[:, s] = jnp.zeros_like(plo[:, s])


def panel_one_kernel(
    s_ref, r_ref, c_ref, got_ref, lh, ll, wh, wl, p_ref, send_ref, ph, plo, inv, inv2
):
    side = s_ref[SLO]
    invert(s_ref, OWN, NC, inv, 18)
    invert(s_ref, OTH, NC, inv2, 18)

    def tile(t, count):
        r = t // NP
        c = t % NP
        dst = (tl(r), tl(c))
        row = NP + side * 6 + r
        p_ref[dst] = r_ref[dst] * s_ref[FILL1 + t].astype(f32)

        @pl.when((inv[row] >= 0) & (inv[c] >= 0))
        def _():
            p_ref[dst] += c_ref[tl(inv[row]), tl(inv[c])]

        hit = (inv2[row] >= 0) & (inv2[c] >= 0)

        @pl.when(hit)
        def _():
            p_ref[dst] += got_ref[count]

        return count + hit.astype(jnp.int32)

    lax.fori_loop(0, 36, tile, 0)
    solve(p_ref, s_ref[LIVE1], lh, ll, wh, wl, ph, plo)
    send_ref[...] = p_ref[:, pl.ds(pl.multiple_of((1 - side) * 384, T), 384)]


def product_kernel(s_ref, p_ref, q_ref, t0_ref, t1_ref, own_ref, cross_ref, ph, plo):
    side = s_ref[SLO]
    ph[...], plo[...] = split(p_ref[...])
    qh, ql = split(q_ref[...])
    mine = pl.ds(pl.multiple_of(side * 384, T), 384)
    pc = (ph[:, mine], plo[:, mine])
    for n in range(3):
        s = slice(n * 256, n * 256 + 256)
        base = jnp.where(side == 0, t0_ref[:, s], t1_ref[:, s])
        own_ref[:, s] = base - dot3((ph[...], plo[...]), (ph[s, :], plo[s, :]), NT)
        base = jnp.where(side == 0, t1_ref[:, s], 0.0)
        cross_ref[:, s] = base - dot3(pc, (qh[s, :], ql[s, :]), NT)


def source_tile(side, inv, inv2, own_ref, cross_ref, c_ref, out_ref, at, r, c):
    i = inv2[r]
    j = inv2[c]
    used = (i >= 0) & (j >= 0)
    i = jnp.maximum(i, 0)
    j = jnp.maximum(j, 0)
    mi = (i // 6) == side
    mj = (j // 6) == side
    li = i % 6
    lj = j % 6

    @pl.when(used & mi & mj)
    def _():
        out_ref[at] = own_ref[tl(li), tl(lj)]

    @pl.when(used & mi & jnp.logical_not(mj))
    def _():
        out_ref[at] = cross_ref[tl(li), tl(lj)]

    @pl.when(used & jnp.logical_not(mi) & mj)
    def _():
        out_ref[at] = cross_ref[tl(lj), tl(li)].T

    @pl.when(jnp.logical_not(used) | (jnp.logical_not(mi) & jnp.logical_not(mj)))
    def _():
        out_ref[at] = jnp.zeros((T, T), f32)

    ci = inv[i + NP]
    cj = inv[j + NP]

    @pl.when(used & (ci >= 0) & (cj >= 0))
    def _():
        out_ref[at] += c_ref[tl(ci), tl(cj)]


def pivot_two_kernel(s_ref, own_ref, cross_ref, c_ref, p_ref, a_ref, b_ref, wide, inv, inv2):
    side = s_ref[SLO]
    quarter = 2 * s_ref[SHI] + side
    invert(s_ref, OWN, NC, inv, 18)
    invert(s_ref, MAP2, NU, inv2, 18)
    wide[...] = jnp.zeros_like(wide)
    wide[pl.ds(pl.multiple_of((quarter % 2) * 64, 64), 192), :] = p_ref[...]
    base = (3 * quarter) // 2

    def emit(out_ref, first, row):
        def col(c, _):
            at = row * (row + 1) // 2 + c - first
            source_tile(side, inv, inv2, own_ref, cross_ref, c_ref, out_ref, at, row, c)

            @pl.when((row >= base) & (row < base + 2))
            def _():
                out_ref[at] += wide[tl(row - base), tl(c)]

            return 0

        lax.fori_loop(0, row + 1, col, 0)

    lax.fori_loop(0, 4, lambda r, _: (emit(a_ref, 0, r), 0)[1], 0)
    lax.fori_loop(4, 6, lambda r, _: (emit(b_ref, 10, r), 0)[1], 0)


def rows_two_kernel(first, width, s_ref, own_ref, cross_ref, c_ref, *refs):
    outs = refs[:4]
    inv, inv2 = refs[4:]
    lo = s_ref[SLO]
    hi = s_ref[SHI]
    invert(s_ref, OWN, NC, inv, 18)
    invert(s_ref, MAP2, NU, inv2, 18)
    half = width // 2
    orders = (
        (0, (1 - hi, 1 - lo), (1 - hi, lo)),
        (0, (hi, 1 - lo), (hi, lo)),
        (half, (1 - hi, 1 - lo), (hi, 1 - lo)),
        (half, (1 - hi, lo), (hi, lo)),
    )
    for out_ref, (skip, one, two) in zip(outs, orders):

        def tile(t, _):
            r = t // half
            later = (r >= 3).astype(jnp.int32)
            a = one[0] + (two[0] - one[0]) * later
            b = one[1] + (two[1] - one[1]) * later
            row = NP + 6 * a + 3 * b + r % 3
            col = first + skip + t % half
            source_tile(lo, inv, inv2, own_ref, cross_ref, c_ref, out_ref, t, row, col)
            return 0

        lax.fori_loop(0, 6 * half, tile, 0)


def rows_two(scalars, own, cross, block_c, first, width, name):
    count = 3 * width
    return call(
        functools.partial(rows_two_kernel, first, width),
        [scalars, own, cross, block_c],
        [None] * 3,
        [shape(count, T, T)] * 4,
        [pltpu.SMEM((18,), jnp.int32)] * 2,
        name,
    )


def panel_two_kernel(
    s_ref, r_ref, xk, x1, x2, zk, z1, z2, lh, ll, wh, wl, p_ref, ph, plo
):
    for r in range(3):
        for c in range(3):
            t = 3 * r + c
            dst = (slice(r * T, r * T + T), slice(c * T, c * T + T))
            fill = s_ref[FILL2 + 6 * r + c].astype(f32)
            p_ref[dst] = r_ref[dst] * fill + ((xk[9 + t] + x1[9 + t]) + x2[t])
            dst = (dst[0], slice((c + 3) * T, (c + 4) * T))
            fill = s_ref[FILL2 + 6 * r + c + 3].astype(f32)
            p_ref[dst] = r_ref[dst] * fill + ((zk[9 + t] + z1[9 + t]) + z2[t])
    solve(p_ref, s_ref[LIVE2], lh, ll, wh, wl, ph, plo)


def schur_kernel(
    s_ref, t0_ref, t1_ref, xk, x1, x2, zk, z1, z2, p_ref, px, pz, pd0, pd1, out_ref
):
    hi = s_ref[SHI]
    lo = s_ref[SLO]
    for r in range(3):
        for c in range(6):
            t = 6 * r + c
            rows = slice(r * T, r * T + T)
            cols = slice(c * T, c * T + T)
            out_ref[rows, cols] = t0_ref[rows, cols] + ((xk[18 + t] + x1[18 + t]) + x2[t])
            right = slice(768 + c * T, 768 + c * T + T)
            out_ref[rows, right] = t1_ref[rows, cols] + ((zk[18 + t] + z1[18 + t]) + z2[t])
    mine = split(p_ref[...])

    def minus(a, b, skip, size, ref):
        cols = pl.ds(pl.multiple_of((2 * a + b) * 384 + skip, 64), size)
        return cols, dot3(mine, split(ref[...]), NT)

    for a, b, ref in ((hi, lo, p_ref), (1 - hi, lo, px), (hi, 1 - lo, pz)):
        cols = pl.ds(pl.multiple_of((2 * a + b) * 384, T), 384)
        out_ref[:, cols] = out_ref[:, cols] - dot3(mine, split(ref[...]), NT)
    diag = jnp.concatenate([pd0[...], pd1[...]], axis=0)
    cols = pl.ds(pl.multiple_of((2 * (1 - hi) + 1 - lo) * 384, T), 384)
    out_ref[:, cols] = out_ref[:, cols] - dot3(mine, split(diag), NT)


def across(axis, values):
    size = lax.axis_size(axis)
    return lax.ppermute(values, axis, [(i, i ^ (size // 2)) for i in range(size)])


def body(
    contribution,
    pivot_one,
    rows_one,
    pivot_two,
    rows_two_in,
    map_one,
    map_two,
    fill_one,
    fill_two,
    live_one,
    live_two,
):
    size_lo = lax.axis_size("lo")
    size_hi = lax.axis_size("hi")
    half_lo = size_lo // 2
    half_hi = size_hi // 2
    lo = lax.axis_index("lo")
    hi = lax.axis_index("hi")
    side_lo = lo // half_lo
    side_hi = hi // half_hi
    front_lo = lo % half_lo
    front_hi = hi % half_hi
    quarter = 2 * side_hi + side_lo
    i32 = jnp.int32
    scalars = jnp.concatenate(
        [
            map_one[hi, lo],
            map_one[hi, (lo + half_lo) % size_lo],
            map_two[hi, front_lo],
            jnp.stack([side_lo, side_hi]).astype(i32),
            live_one[hi, front_lo][None],
            live_two[front_hi, front_lo][None],
            lax.dynamic_slice_in_dim(fill_one[hi, front_lo], side_lo * 6, 6, 0).reshape(36),
            lax.dynamic_slice_in_dim(fill_two[front_hi, front_lo], quarter * 3, 3, 0).reshape(18),
        ]
    )
    c = contribution[0, 0]
    rows1 = rows_one[0, 0]
    rows2 = rows_two_in[0, 0]
    smem = pltpu.SMEM((18,), i32)
    n = NP * T

    piv, coup = call(
        gather_one_kernel,
        [scalars, c, pivot_one[0, 0]],
        [None, None],
        [shape(21, T, T), shape(16, T, T)],
        [smem],
        "gather_one",
    )
    piv_got = across("lo", piv)
    coup, piv_got = lax.optimization_barrier((coup, piv_got))
    coup_got = across("lo", coup)
    lower_one, *fac1 = factor(
        scalars, [(piv, piv_got)], LIVE1, lambda s: s[SLO] * 384, 384, "factor_one"
    )
    panel_one, send = call(
        panel_one_kernel,
        [scalars, rows1, c, coup_got, *fac1],
        [block(n, n, 0)] + [None] * 6,
        [shape(n, n), shape(n, n // 2)],
        [pltpu.VMEM((n, n), bf16)] * 2 + [smem] * 2,
        "panel_one",
        flops=3_000_000_000,
    )
    got = across("lo", send)
    own, cross = call(
        product_kernel,
        [scalars, panel_one, got, rows1, rows1],
        [None, None, block(n, n, 1), block(n, n, 2)],
        [shape(n, n), shape(n, n)],
        [pltpu.VMEM((n, n), bf16)] * 2,
        "product_one",
        flops=4_000_000_000,
    )
    pa, pb = call(
        pivot_two_kernel,
        [scalars, own, cross, c, pivot_two[0, 0]],
        [None] * 4,
        [shape(10, T, T), shape(11, T, T)],
        [pltpu.VMEM((2 * T, n), f32), smem, smem],
        "pivot_two",
    )
    pa1 = across("hi", pa)
    pb1 = across("lo", pb)
    cxs, cxk, czs, czk = rows_two(scalars, own, cross, c, 0, NP, "coupling_two")
    cx1 = across("hi", cxs)
    cz1 = across("lo", czs)
    pa = pa + pa1
    pb = pb + pb1
    pa2 = across("lo", pa)
    pb2 = across("hi", pb)
    txs, txk, tzs, tzk = rows_two(scalars, own, cross, c, NP, NU, "trailing_two")
    tx1 = across("hi", txs)
    tz1 = across("lo", tzs)
    cx2 = across("lo", cxk[:9] + cx1[:9])
    cz2 = across("hi", czk[:9] + cz1[:9])
    lower_two, *fac2 = factor(
        scalars,
        [(pa, pa2), (pb, pb2)],
        LIVE2,
        lambda s: (2 * s[SHI] + s[SLO]) * 192,
        192,
        "factor_two",
    )
    (panel_two,) = call(
        panel_two_kernel,
        [scalars, rows2, cxk, cx1, cx2, czk, cz1, cz2, *fac2],
        [block(384, n, 0)] + [None] * 10,
        [shape(384, n)],
        [pltpu.VMEM((384, n), bf16)] * 2,
        "panel_two",
        flops=2_000_000_000,
    )
    tx2 = across("lo", txk[:18] + tx1[:18])
    tz2 = across("hi", tzk[:18] + tz1[:18])
    px = across("hi", panel_two)
    pz = across("lo", panel_two)
    pd0 = across("hi", pz[:192])
    pd1 = across("lo", px[192:])
    (schur_two,) = call(
        schur_kernel,
        [scalars, rows2, rows2, txk, tx1, tx2, tzk, tz1, tz2, panel_two, px, pz, pd0, pd1],
        [block(384, n, 1), block(384, n, 2)] + [None] * 11,
        [shape(384, NU * T)],
        [],
        "schur_two",
        flops=3_000_000_000,
    )
    return tuple(
        out[None, None] for out in (lower_one, panel_one, lower_two, panel_two, schur_two)
    )


def solution(mesh):
    split_spec = P("hi", "lo", None, None)
    return jax.shard_map(
        body,
        mesh=mesh,
        in_specs=(split_spec,) * 5 + (P(),) * 6,
        out_specs=(split_spec,) * 5,
        check_vma=False,
    )
```

```python
import functools
import jax
import jax.numpy as jnp
from jax import lax
from jax.experimental import pallas as pl
from jax.experimental.pallas import tpu as pltpu
from jax.sharding import PartitionSpec as P

T = 128
NP = 6
NU = 12
NC = 8
f32 = jnp.float32
bf16 = jnp.bfloat16
NN = ((1,), (0,))
NT = ((1,), (1,))
OWN, OTH, MAP2, SLO, SHI, LIVE1, LIVE2, FILL1, FILL2 = 0, 8, 16, 28, 29, 30, 31, 32, 68


def tl(i):
    return pl.ds(pl.multiple_of(i * T, T), T)


def split(x):
    hi = x.astype(bf16)
    return hi, (x - hi.astype(f32)).astype(bf16)


def dot3(a, b, dims):
    (ah, al), (bh, bl) = a, b
    dn = (dims, ((), ()))
    f = lambda x, y: lax.dot_general(x, y, dn, preferred_element_type=f32)
    return f(ah, bh) + (f(ah, bl) + f(al, bh))


def call(kernel, args, specs, outs, scratch, name, flops=0, grid=(1,)):
    whole = pl.BlockSpec(memory_space=pltpu.VMEM)
    in_specs = [whole if s is None else s for s in specs]
    nbytes = sum(4 * a.size for a in args[1:]) + sum(4 * o.size for o in outs)
    return pl.pallas_call(
        kernel,
        grid_spec=pltpu.PrefetchScalarGridSpec(
            num_scalar_prefetch=1,
            grid=grid,
            in_specs=in_specs,
            out_specs=[whole] * len(outs),
            scratch_shapes=scratch,
        ),
        out_shape=outs,
        compiler_params=pltpu.CompilerParams(vmem_limit_bytes=60 * 1024 * 1024),
        cost_estimate=pl.CostEstimate(flops=flops, bytes_accessed=nbytes, transcendentals=0),
        name=name,
    )(*args)


def shape(*dims, dtype=f32):
    return jax.ShapeDtypeStruct(dims, dtype)


def block(rows, cols, j):
    return pl.BlockSpec((rows, cols), lambda i, s: (0, j))


def invert(s_ref, first, count, inv_ref, size):
    for r in range(size):
        inv_ref[r] = -1
    for i in range(count):
        inv_ref[s_ref[first + i]] = i


def gather_one_kernel(half_lo, s_ref, c_ref, p_ref, piv_ref, coup_ref, inv):
    side = lax.axis_index("lo") // half_lo
    invert(s_ref, OWN, NC, inv, 18)

    def piv_row(r, _):
        local = r - 3 * side

        def piv_col(c, _):
            at = r * (r + 1) // 2 + c

            @pl.when((local >= 0) & (local < 3))
            def _():
                piv_ref[at] = p_ref[tl(local), tl(c)]

            @pl.when((local < 0) | (local >= 3))
            def _():
                piv_ref[at] = jnp.zeros((T, T), f32)

            @pl.when((inv[r] >= 0) & (inv[c] >= 0))
            def _():
                piv_ref[at] += c_ref[tl(inv[r]), tl(inv[c])]

            return 0

        return lax.fori_loop(0, r + 1, piv_col, 0)

    lax.fori_loop(0, NP, piv_row, 0)

    def coup_tile(t, count):
        row = inv[NP + (1 - side) * 6 + t // NP]
        col = inv[t % NP]
        hit = (row >= 0) & (col >= 0)

        @pl.when(hit)
        def _():
            coup_ref[count] = c_ref[tl(row), tl(col)]

        return count + hit.astype(jnp.int32)

    lax.fori_loop(0, 36, coup_tile, 0)


def factor_tile(d_ref, w_ref, u_ref):
    lane = lax.broadcasted_iota(jnp.int32, (8, T), 1)
    row = lax.broadcasted_iota(jnp.int32, (8, T), 0)
    for g in range(16):
        r0 = 8 * g
        w_ref[r0 : r0 + 8, :] = jnp.where(lane == row + r0, 1.0, 0.0).astype(f32)
    for g in range(16):
        r0 = 8 * g
        rows = [jnp.broadcast_to(d_ref[r0 + i : r0 + i + 1, :], (8, T)) for i in range(8)]
        wrows = [jnp.broadcast_to(w_ref[r0 + i : r0 + i + 1, :], (8, T)) for i in range(8)]
        e = [
            [jnp.broadcast_to(rows[i][:, r0 + k : r0 + k + 1], (8, T)) for k in range(i + 1)]
            for i in range(8)
        ]
        l = [[None] * 8 for _ in range(8)]
        rinv = [None] * 8
        for j in range(8):
            rinv[j] = lax.rsqrt(e[j][j])
            for i in range(j + 1, 8):
                l[i][j] = e[i][j] * rinv[j]
            for i in range(j + 1, 8):
                for k in range(j + 1, i + 1):
                    e[i][k] = e[i][k] - l[i][j] * l[k][j]
        u = [None] * 8
        w = [None] * 8
        for j in range(8):
            a = rows[j]
            b = wrows[j]
            for k in range(j):
                a = a - l[j][k] * u[k]
                b = b - l[j][k] * w[k]
            u[j] = a * rinv[j]
            w[j] = b * rinv[j]
            u_ref[r0 + j : r0 + j + 1, :] = jnp.where(lane[:1] >= r0 + j, u[j][:1], 0.0)
            w_ref[r0 + j : r0 + j + 1, :] = w[j][:1]
        for r in range(g + 1, 16):
            q = 8 * r
            dr = d_ref[q : q + 8, :]
            wr = w_ref[q : q + 8, :]
            c = [jnp.broadcast_to(dr[:, r0 + k : r0 + k + 1], (8, T)) for k in range(8)]
            for j in range(8):
                a = c[j]
                for k in range(j):
                    a = a - l[j][k] * c[k]
                c[j] = a * rinv[j]
            for j in range(8):
                dr = dr - c[j] * u[j]
                wr = wr - c[j] * w[j]
            d_ref[q : q + 8, :] = dr
            w_ref[q : q + 8, :] = wr


def factor_kernel(counts, live_at, take, s_ref, *refs):
    n_in = 2 * len(counts)
    ins = refs[:n_in]
    low_ref, lh_ref, ll_ref, wh_ref, wl_ref, a_s, l_s, d_s, w_s, u_s = refs[n_in:]
    live = s_ref[live_at]
    first = 0
    spots = [(r, c) for r in range(NP) for c in range(r + 1)]
    for n, count in enumerate(counts):
        for t in range(count):
            r, c = spots[first + t]
            a_s[r * T : r * T + T, c * T : c * T + T] = ins[2 * n][t] + ins[2 * n + 1][t]
        first += count
    l_s[...] = jnp.zeros_like(l_s)
    ii = lax.broadcasted_iota(jnp.int32, (T, T), 0)
    jj = lax.broadcasted_iota(jnp.int32, (T, T), 1)
    eye = jnp.where(ii == jj, 1.0, 0.0).astype(f32)

    def dead(k, _):
        l_s[tl(k), tl(k)] = eye
        return 0

    lax.fori_loop(live, NP, dead, 0)
    tile_row = lax.broadcasted_iota(jnp.int32, (NP * T, T), 0) // T

    def step(k, _):
        s = tl(k)
        d_s[...] = a_s[s, s]
        factor_tile(d_s, w_s, u_s)
        w = split(w_s[...])
        wh_ref[s, :] = w[0]
        wl_ref[s, :] = w[1]

        x = dot3(split(a_s[:, s]), w, NT)
        lh_ref[:, s], ll_ref[:, s] = split(x)
        l_s[:, s] = jnp.where((tile_row > k) & (tile_row < live), x, 0.0)
        l_s[s, s] = u_s[...].T

        def col(j, _):
            xj = (lh_ref[tl(j), s], ll_ref[tl(j), s])
            a_s[:, tl(j)] = a_s[:, tl(j)] - dot3((lh_ref[:, s], ll_ref[:, s]), xj, NT)
            return 0

        return lax.fori_loop(k + 1, live, col, 0)

    lax.fori_loop(0, live, step, 0)
    low_ref[...] = l_s[pl.ds(pl.multiple_of(take(s_ref), 64), low_ref.shape[0]), :]


def factor(scalars, pairs, live_at, take, rows, name):
    counts = tuple(x.shape[0] for x, _ in pairs)
    n = NP * T
    return call(
        functools.partial(factor_kernel, counts, live_at, take),
        [scalars] + [x for pair in pairs for x in pair],
        [None] * (2 * len(pairs)),
        [shape(rows, n), shape(n, n, dtype=bf16), shape(n, n, dtype=bf16)]
        + [shape(n, T, dtype=bf16)] * 2,
        [pltpu.VMEM((n, n), f32)] * 2 + [pltpu.VMEM((T, T), f32)] * 3,
        name,
        flops=20_000_000_000,
    )


def solve(x_ref, live, lh_ref, ll_ref, wh_ref, wl_ref, ph, plo):
    for k in range(NP):
        s = slice(k * T, k * T + T)

        @pl.when(k < live)
        def _():
            x = x_ref[:, s]
            if k:
                b = slice(0, k * T)
                x = x - dot3((ph[:, b], plo[:, b]), (lh_ref[s, b], ll_ref[s, b]), NT)
            x = dot3(split(x), (wh_ref[s, :], wl_ref[s, :]), NT)
            x_ref[:, s] = x
            xh, xl = split(x)
            ph[:, s] = xh
            plo[:, s] = xl

        @pl.when(k >= live)
        def _():
            x_ref[:, s] = jnp.zeros_like(x_ref[:, s])
            ph[:, s] = jnp.zeros_like(ph[:, s])
            plo[:, s] = jnp.zeros_like(plo[:, s])


def couple_one_kernel(s_ref, r_ref, c_ref, x_ref, inv):
    side = s_ref[SLO]
    invert(s_ref, OWN, NC, inv, 18)

    def tile(t, _):
        r = t // NP
        c = t % NP
        dst = (tl(r), tl(c))
        row = NP + side * 6 + r
        x_ref[dst] = r_ref[dst] * s_ref[FILL1 + t].astype(f32)

        @pl.when((inv[row] >= 0) & (inv[c] >= 0))
        def _():
            x_ref[dst] += c_ref[tl(inv[row]), tl(inv[c])]

        return 0

    lax.fori_loop(0, 36, tile, 0)


def panel_one_kernel(s_ref, x_ref, got_ref, lh, ll, wh, wl, p_ref, send_ref, ph, plo, inv2):
    side = s_ref[SLO]
    invert(s_ref, OTH, NC, inv2, 18)
    p_ref[...] = x_ref[...]

    def tile(t, count):
        r = t // NP
        c = t % NP
        row = NP + side * 6 + r
        hit = (inv2[row] >= 0) & (inv2[c] >= 0)

        @pl.when(hit)
        def _():
            p_ref[tl(r), tl(c)] += got_ref[count]

        return count + hit.astype(jnp.int32)

    lax.fori_loop(0, 36, tile, 0)
    solve(p_ref, s_ref[LIVE1], lh, ll, wh, wl, ph, plo)
    send_ref[...] = p_ref[:, pl.ds(pl.multiple_of((1 - side) * 384, T), 384)]


def own_kernel(s_ref, p_ref, t0_ref, t1_ref, own_ref, ph, plo):
    side = s_ref[SLO]
    ph[...], plo[...] = split(p_ref[...])
    for n in range(3):
        s = slice(n * 256, n * 256 + 256)
        base = jnp.where(side == 0, t0_ref[:, s], t1_ref[:, s])
        own_ref[:, s] = base - dot3((ph[...], plo[...]), (ph[s, :], plo[s, :]), NT)


def source_tile(side, inv, inv2, own_ref, cross_ref, c_ref, out_ref, at, r, c):
    i = inv2[r]
    j = inv2[c]
    used = (i >= 0) & (j >= 0)
    i = jnp.maximum(i, 0)
    j = jnp.maximum(j, 0)
    mi = (i // 6) == side
    mj = (j // 6) == side
    li = i % 6
    lj = j % 6

    @pl.when(used & mi & mj)
    def _():
        out_ref[at] = own_ref[tl(li), tl(lj)]

    @pl.when(used & mi & jnp.logical_not(mj))
    def _():
        out_ref[at] = cross_ref[tl(li), tl(lj)]

    @pl.when(used & jnp.logical_not(mi) & mj)
    def _():
        out_ref[at] = cross_ref[tl(lj), tl(li)].T

    @pl.when(jnp.logical_not(used) | (jnp.logical_not(mi) & jnp.logical_not(mj)))
    def _():
        out_ref[at] = jnp.zeros((T, T), f32)

    ci = inv[i + NP]
    cj = inv[j + NP]

    @pl.when(used & (ci >= 0) & (cj >= 0))
    def _():
        out_ref[at] += c_ref[tl(ci), tl(cj)]


def cross_kernel(
    s_ref, p_ref, q_ref, t1_ref, own_ref, c_ref, pv_ref, cross_ref, a_ref, b_ref, wide, inv, inv2
):
    side = s_ref[SLO]
    quarter = 2 * s_ref[SHI] + side
    mine = pl.ds(pl.multiple_of(side * 384, T), 384)
    pc = split(p_ref[:, mine])
    qh, ql = split(q_ref[...])
    for n in range(3):
        s = slice(n * 256, n * 256 + 256)
        base = jnp.where(side == 0, t1_ref[:, s], 0.0)
        cross_ref[:, s] = base - dot3(pc, (qh[s, :], ql[s, :]), NT)
    invert(s_ref, OWN, NC, inv, 18)
    invert(s_ref, MAP2, NU, inv2, 18)
    wide[...] = jnp.zeros_like(wide)
    wide[pl.ds(pl.multiple_of((quarter % 2) * 64, 64), 192), :] = pv_ref[...]
    base = (3 * quarter) // 2

    def emit(out_ref, first, row):
        def col(c, _):
            at = row * (row + 1) // 2 + c - first
            source_tile(side, inv, inv2, own_ref, cross_ref, c_ref, out_ref, at, row, c)

            @pl.when((row >= base) & (row < base + 2))
            def _():
                out_ref[at] += wide[tl(row - base), tl(c)]

            return 0

        lax.fori_loop(0, row + 1, col, 0)

    lax.fori_loop(0, 4, lambda r, _: (emit(a_ref, 0, r), 0)[1], 0)
    lax.fori_loop(4, 6, lambda r, _: (emit(b_ref, 10, r), 0)[1], 0)


def rows_two_kernel(first, width, s_ref, own_ref, cross_ref, c_ref, *refs):
    outs = refs[:4]
    inv, inv2 = refs[4:]
    lo = s_ref[SLO]
    hi = s_ref[SHI]
    invert(s_ref, OWN, NC, inv, 18)
    invert(s_ref, MAP2, NU, inv2, 18)
    half = width // 2
    orders = (
        (0, (1 - hi, 1 - lo), (1 - hi, lo)),
        (0, (hi, 1 - lo), (hi, lo)),
        (half, (1 - hi, 1 - lo), (hi, 1 - lo)),
        (half, (1 - hi, lo), (hi, lo)),
    )
    for out_ref, (skip, one, two) in zip(outs, orders):

        def tile(t, _):
            r = t // half
            later = (r >= 3).astype(jnp.int32)
            a = one[0] + (two[0] - one[0]) * later
            b = one[1] + (two[1] - one[1]) * later
            row = NP + 6 * a + 3 * b + r % 3
            col = first + skip + t % half
            source_tile(lo, inv, inv2, own_ref, cross_ref, c_ref, out_ref, t, row, col)
            return 0

        lax.fori_loop(0, 6 * half, tile, 0)


def rows_two(scalars, own, cross, block_c, first, width, name):
    count = 3 * width
    return call(
        functools.partial(rows_two_kernel, first, width),
        [scalars, own, cross, block_c],
        [None] * 3,
        [shape(count, T, T)] * 4,
        [pltpu.SMEM((18,), jnp.int32)] * 2,
        name,
    )


NINE = [(r, c) for r in range(3) for c in range(3)]
DX, DZ = [(0, 0), (1, 0), (1, 1)], [(2, 0), (2, 1), (2, 2)]
GX, GZ = NINE[:4], NINE[4:]


def chain_x(m, x, z, d):
    return (
        [(z, z, t) for t in DX]
        + [(z, x, t) for t in GX]
        + [(m, z, t) for t in NINE]
        + [(m, m, t) for t in DX]
        + [(m, d, t) for t in GX]
    )


def chain_z(m, x, z, d):
    return (
        [(x, x, t) for t in DZ]
        + [(x, z, t) for t in GZ]
        + [(m, x, t) for t in NINE]
        + [(m, m, t) for t in DZ]
        + [(m, d, t) for t in GZ]
    )


def trailing_two_kernel(
    s_ref, own_ref, cross_ref, c_ref, xs, xk, zs, zk, inv, inv2, rtab, ctab
):
    lo = s_ref[SLO]
    hi = s_ref[SHI]
    invert(s_ref, OWN, NC, inv, 18)
    invert(s_ref, MAP2, NU, inv2, 18)
    m, x, z, d = (
        NP + 3 * (2 * a + b) for a, b in ((hi, lo), (1 - hi, lo), (hi, 1 - lo), (1 - hi, 1 - lo))
    )
    for out_ref, tiles in (
        (xs, chain_x(x, m, d, z)),
        (xk, chain_x(m, x, z, d)),
        (zs, chain_z(z, d, m, x)),
        (zk, chain_z(m, x, z, d)),
    ):
        for n, (rq, cq, (r, c)) in enumerate(tiles):
            rtab[n] = rq + r
            ctab[n] = cq + c

        def tile(t, _):
            source_tile(lo, inv, inv2, own_ref, cross_ref, c_ref, out_ref, t, rtab[t], ctab[t])
            return 0

        lax.fori_loop(0, len(tiles), tile, 0)


def panel_two_kernel(
    s_ref, r_ref, xk, x1, x2, zk, z1, z2, lh, ll, wh, wl, p_ref, ph, plo
):
    for r in range(3):
        for c in range(3):
            t = 3 * r + c
            dst = (slice(r * T, r * T + T), slice(c * T, c * T + T))
            fill = s_ref[FILL2 + 6 * r + c].astype(f32)
            p_ref[dst] = r_ref[dst] * fill + ((xk[9 + t] + x1[9 + t]) + x2[t])
            dst = (dst[0], slice((c + 3) * T, (c + 4) * T))
            fill = s_ref[FILL2 + 6 * r + c + 3].astype(f32)
            p_ref[dst] = r_ref[dst] * fill + ((zk[9 + t] + z1[9 + t]) + z2[t])
    solve(p_ref, s_ref[LIVE2], lh, ll, wh, wl, ph, plo)


def schur_base_kernel(s_ref, r_ref, p_ref, xk, x1, x2, zk, z1, z2, out_ref):
    hi = s_ref[SHI]
    lo = s_ref[SLO]
    out_ref[...] = r_ref[:, NP * T :]
    m, x, z, d = (
        3 * (2 * a + b) for a, b in ((hi, lo), (1 - hi, lo), (hi, 1 - lo), (1 - hi, 1 - lo))
    )
    mine = split(p_ref[...])
    cols = pl.ds(pl.multiple_of(m * T, T), 384)
    out_ref[:, cols] = out_ref[:, cols] - dot3(mine, mine, NT)

    def add(quarter, r, c, value):
        out_ref[r * T : r * T + T, tl(quarter + c)] += value

    for k, r1, r2, diag, cross, pair in ((xk, x1, x2, DX, GX, z), (zk, z1, z2, DZ, GZ, x)):
        nd = len(diag)
        ng = len(cross)
        base = nd + ng + 9
        for n, (r, c) in enumerate(diag):
            v = (k[base + n] + r1[base + n]) + r2[n]
            add(m, r, c, v)
            if r != c:
                add(m, c, r, v.T)
        for n, (r, c) in enumerate(cross):
            v = (k[base + nd + n] + r1[base + nd + n]) + r2[nd + n]
            add(d, r, c, v)
        for n, (r, c) in enumerate(NINE):
            v = (k[nd + ng + n] + r1[nd + ng + n]) + r2[nd + ng + 3 * c + r].T
            add(pair, r, c, v)


def schur_kernel(s_ref, b_ref, p_ref, px, pz, pd0, pd1, out_ref):
    hi = s_ref[SHI]
    lo = s_ref[SLO]
    mine = split(p_ref[...])

    def minus(a, b, other):
        cols = pl.ds(pl.multiple_of((2 * a + b) * 384, T), 384)
        out_ref[:, cols] = b_ref[:, cols] - dot3(mine, split(other), NT)

    minus(1 - hi, lo, px[...])
    minus(hi, 1 - lo, pz[...])
    minus(1 - hi, 1 - lo, jnp.concatenate([pd0[...], pd1[...]], axis=0))
    cols = pl.ds(pl.multiple_of((2 * hi + lo) * 384, T), 384)
    out_ref[:, cols] = b_ref[:, cols]


def across(axis, values):
    size = lax.axis_size(axis)
    return lax.ppermute(values, axis, [(i, i ^ (size // 2)) for i in range(size)])


def body(
    contribution,
    pivot_one,
    rows_one,
    pivot_two,
    rows_two_in,
    map_one,
    map_two,
    fill_one,
    fill_two,
    live_one,
    live_two,
):
    size_lo = lax.axis_size("lo")
    size_hi = lax.axis_size("hi")
    half_lo = size_lo // 2
    half_hi = size_hi // 2
    lo = lax.axis_index("lo")
    hi = lax.axis_index("hi")
    side_lo = lo // half_lo
    side_hi = hi // half_hi
    front_lo = lo % half_lo
    front_hi = hi % half_hi
    quarter = 2 * side_hi + side_lo
    i32 = jnp.int32
    c = contribution[0, 0]
    rows1 = rows_one[0, 0]
    rows2 = rows_two_in[0, 0]
    smem = pltpu.SMEM((18,), i32)
    n = NP * T

    piv, coup = call(
        functools.partial(gather_one_kernel, half_lo),
        [map_one[hi, lo], c, pivot_one[0, 0]],
        [None, None],
        [shape(21, T, T), shape(16, T, T)],
        [smem],
        "gather_one",
    )
    piv, map_one, map_two, fill_one, fill_two, live_one, live_two = lax.optimization_barrier(
        (piv, map_one, map_two, fill_one, fill_two, live_one, live_two)
    )
    piv_got = across("lo", piv)
    scalars = jnp.concatenate(
        [
            map_one[hi, lo],
            map_one[hi, (lo + half_lo) % size_lo],
            map_two[hi, front_lo],
            jnp.stack([side_lo, side_hi]).astype(i32),
            live_one[hi, front_lo][None],
            live_two[front_hi, front_lo][None],
            lax.dynamic_slice_in_dim(fill_one[hi, front_lo], side_lo * 6, 6, 0).reshape(36),
            lax.dynamic_slice_in_dim(fill_two[front_hi, front_lo], quarter * 3, 3, 0).reshape(18),
        ]
    )
    (x_one,) = call(
        couple_one_kernel,
        [scalars, rows1, c],
        [block(n, n, 0), None],
        [shape(n, n)],
        [smem],
        "couple_one",
    )
    coup, piv_got = lax.optimization_barrier((coup, piv_got))
    coup_got = across("lo", coup)
    lower_one, *fac1 = factor(
        scalars, [(piv, piv_got)], LIVE1, lambda s: s[SLO] * 384, 384, "factor_one"
    )
    panel_one, send = call(
        panel_one_kernel,
        [scalars, x_one, coup_got, *fac1],
        [None] * 6,
        [shape(n, n), shape(n, n // 2)],
        [pltpu.VMEM((n, n), bf16)] * 2 + [smem],
        "panel_one",
        flops=3_000_000_000,
    )
    got = across("lo", send)
    (own,) = call(
        own_kernel,
        [scalars, panel_one, rows1, rows1],
        [None, block(n, n, 1), block(n, n, 2)],
        [shape(n, n)],
        [pltpu.VMEM((n, n), bf16)] * 2,
        "own_one",
        flops=4_000_000_000,
    )
    cross, pa, pb = call(
        cross_kernel,
        [scalars, panel_one, got, rows1, own, c, pivot_two[0, 0]],
        [None, None, block(n, n, 2), None, None, None],
        [shape(n, n), shape(10, T, T), shape(11, T, T)],
        [pltpu.VMEM((2 * T, n), f32), smem, smem],
        "cross_one",
        flops=2_000_000_000,
    )
    pa1 = across("hi", pa)
    pb1 = across("lo", pb)
    pa, pb, cross = lax.optimization_barrier((pa, pb, cross))
    cxs, cxk, czs, czk = rows_two(scalars, own, cross, c, 0, NP, "coupling_two")
    pa = pa + pa1
    pb = pb + pb1
    pa, pb, cxs, czs = lax.optimization_barrier((pa, pb, cxs, czs))
    pa2 = across("lo", pa)
    pb2 = across("hi", pb)
    cx1 = across("hi", cxs)
    cz1 = across("lo", czs)
    txs, txk, tzs, tzk = call(
        trailing_two_kernel,
        [scalars, own, cross, c],
        [None] * 3,
        [shape(23, T, T)] * 2 + [shape(25, T, T)] * 2,
        [smem, smem] + [pltpu.SMEM((32,), i32)] * 2,
        "trailing_two",
    )
    tx1 = across("hi", txs)
    tz1 = across("lo", tzs)
    lower_two, *fac2 = factor(
        scalars,
        [(pa, pa2), (pb, pb2)],
        LIVE2,
        lambda s: (2 * s[SHI] + s[SLO]) * 192,
        192,
        "factor_two",
    )
    cx2 = across("lo", cxk[:9] + cx1[:9])
    cz2 = across("hi", czk[:9] + cz1[:9])
    (panel_two,) = call(
        panel_two_kernel,
        [scalars, rows2, cxk, cx1, cx2, czk, cz1, cz2, *fac2],
        [block(384, n, 0)] + [None] * 10,
        [shape(384, n)],
        [pltpu.VMEM((384, n), bf16)] * 2,
        "panel_two",
        flops=2_000_000_000,
    )
    tx2 = across("lo", txk[:16] + tx1[:16])
    tz2 = across("hi", tzk[:17] + tz1[:17])
    px = across("hi", panel_two)
    pz = across("lo", panel_two)
    pd0 = across("hi", pz[:192])
    pd1 = across("lo", px[192:])
    (base_two,) = call(
        schur_base_kernel,
        [scalars, rows2, panel_two, txk, tx1, tx2, tzk, tz1, tz2],
        [None] * 8,
        [shape(384, NU * T)],
        [],
        "schur_base",
        flops=1_000_000_000,
    )
    (schur_two,) = call(
        schur_kernel,
        [scalars, base_two, panel_two, px, pz, pd0, pd1],
        [None] * 6,
        [shape(384, NU * T)],
        [],
        "schur_two",
        flops=3_000_000_000,
    )
    return tuple(
        out[None, None] for out in (lower_one, panel_one, lower_two, panel_two, schur_two)
    )


def solution(mesh):
    split_spec = P("hi", "lo", None, None)
    return jax.shard_map(
        body,
        mesh=mesh,
        in_specs=(split_spec,) * 5 + (P(),) * 6,
        out_specs=(split_spec,) * 5,
        check_vma=False,
    )
```

```python
import functools
import jax
import jax.numpy as jnp
from jax import lax
from jax.experimental import pallas as pl
from jax.experimental.pallas import tpu as pltpu
from jax.sharding import PartitionSpec as P


T = 128
NP = 6
NU = 12
NC = 8
f32 = jnp.float32
bf16 = jnp.bfloat16
NT = ((1,), (1,))
OWN, OTH, MAP2, SLO, SHI, LIVE1, LIVE2, FILL1, FILL2 = 0, 8, 16, 28, 29, 30, 31, 32, 68


def tl(i):
    if isinstance(i, int):
        return slice(i * T, i * T + T)
    return pl.ds(pl.multiple_of(i * T, T), T)


def split(x):
    hi = x.astype(bf16)
    return hi, (x - hi.astype(f32)).astype(bf16)


def dot3(a, b, dims):
    (ah, al), (bh, bl) = a, b
    dn = (dims, ((), ()))
    f = lambda x, y: lax.dot_general(x, y, dn, preferred_element_type=f32)
    return f(ah, bh) + (f(ah, bl) + f(al, bh))


def call(kernel, args, specs, outs, scratch, flops=0, grid=(1,)):
    whole = pl.BlockSpec(memory_space=pltpu.VMEM)
    in_specs = [whole if s is None else s for s in specs]
    nbytes = sum(4 * a.size for a in args[1:]) + sum(4 * o.size for o in outs)
    return pl.pallas_call(
        kernel,
        grid_spec=pltpu.PrefetchScalarGridSpec(
            num_scalar_prefetch=1,
            grid=grid,
            in_specs=in_specs,
            out_specs=[whole] * len(outs),
            scratch_shapes=scratch,
        ),
        out_shape=outs,
        compiler_params=pltpu.CompilerParams(vmem_limit_bytes=60 * 1024 * 1024),
        cost_estimate=pl.CostEstimate(flops=flops, bytes_accessed=nbytes, transcendentals=0),
    )(*args)


def shape(*dims, dtype=f32):
    return jax.ShapeDtypeStruct(dims, dtype)


def block(rows, cols, j):
    return pl.BlockSpec((rows, cols), lambda i, s: (0, j))


def invert(s_ref, first, count, inv_ref, size):
    for r in range(size):
        inv_ref[r] = -1
    for i in range(count):
        inv_ref[s_ref[first + i]] = i


def gather_one_kernel(half_lo, s_ref, c_ref, p_ref, a_ref, b_ref, coup_ref, inv):
    side = lax.axis_index("lo") // half_lo
    invert(s_ref, OWN, NC, inv, 18)

    for c in range(NP):
        out_ref = a_ref if c < 2 else b_ref
        base = BY_COL.index((c, c)) - (0 if c < 2 else 11) - c

        def tile(r, _):
            at = base + r
            local = r - 3 * side

            @pl.when((local >= 0) & (local < 3))
            def _():
                out_ref[at] = p_ref[tl(local), tl(c)]

            @pl.when((local < 0) | (local >= 3))
            def _():
                out_ref[at] = jnp.zeros((T, T), f32)

            @pl.when((inv[r] >= 0) & (inv[c] >= 0))
            def _():
                out_ref[at] += c_ref[tl(inv[r]), tl(inv[c])]

            return 0

        lax.fori_loop(c, NP, tile, 0)

    def coup_tile(t, count):
        row = inv[NP + (1 - side) * 6 + t // NP]
        col = inv[t % NP]
        hit = (row >= 0) & (col >= 0)

        @pl.when(hit)
        def _():
            coup_ref[count] = c_ref[tl(row), tl(col)]

        return count + hit.astype(jnp.int32)

    lax.fori_loop(0, 36, coup_tile, 0)


def factor_tile(x_ref, w_ref, u_ref):
    lane = lax.broadcasted_iota(jnp.int32, (8, T), 1)
    wide = lambda v: jnp.broadcast_to(v, (8, T))
    cols = lambda x, r0: [wide(x[:, r0 + k : r0 + k + 1]) for k in range(8)]
    diag = cols(x_ref[0:8, :], 0)
    x = x_ref[8:16, :]
    ahead = (cols(x, 0), cols(x, 8))
    for g in range(16):
        r0 = 8 * g
        inside = (lane >= r0) & (lane < r0 + 8)
        e = [[wide(diag[k][i : i + 1, :]) for k in range(i + 1)] for i in range(8)]
        l = [[None] * 8 for _ in range(8)]
        rinv = [None] * 8
        for j in range(8):
            rinv[j] = lax.rsqrt(e[j][j])
            l[j][j] = e[j][j] * rinv[j]
            for i in range(j + 1, 8):
                l[i][j] = e[i][j] * rinv[j]
            for i in range(j + 1, 8):
                for k in range(j + 1, i + 1):
                    e[i][k] = e[i][k] - l[i][j] * l[k][j]

        def eliminate(c):
            for j in range(8):
                a = c[j]
                for k in range(j):
                    a = a - l[j][k] * c[k]
                c[j] = a * rinv[j]
            return c

        if g < 15:
            c1 = eliminate(ahead[0])
            diag = ahead[1]
            for j in range(8):
                for k in range(8):
                    diag[k] = diag[k] - c1[j] * wide(c1[j][k : k + 1, :])
        z = [None] * 8
        for j in range(8):
            row = wide(x_ref[r0 + j : r0 + j + 1, :])
            a = jnp.where(inside, jnp.where(lane == r0 + j, 1.0, 0.0), row)
            for k in range(j):
                a = a - l[j][k] * z[k]
            z[j] = a * rinv[j]
            d = jnp.where(lane < r0, 0.0, z[j])
            for k in range(j, 8):
                d = jnp.where(lane == r0 + k, l[k][j], d)
            if j:
                d = jnp.where(lane < r0 + j, 0.0, d)
            u_ref[r0 + j : r0 + j + 1, :] = d[:1]
            w_ref[r0 + j : r0 + j + 1, :] = jnp.where(lane < r0 + 8, z[j], 0.0)[:1]
        y = [None] * 8
        for j in reversed(range(8)):
            a = z[j]
            for i in range(j + 1, 8):
                a = a - l[i][j] * y[i]
            y[j] = a * rinv[j]
        for r in range(g + 1, 16):
            q = 8 * r
            x = x_ref[q : q + 8, :]
            if r == g + 1:
                c, v = c1, z
            else:
                c, v = cols(x, r0), y
            x = jnp.where(inside, 0.0, x)
            for j in range(8):
                x = x - c[j] * v[j]
            x_ref[q : q + 8, :] = x
            if r == g + 2:
                ahead = (cols(x, r0 + 8), cols(x, r0 + 16))


BY_ROW = [(r, c) for r in range(NP) for c in range(r + 1)]
BY_COL = [(r, c) for c in range(NP) for r in range(c, NP)]


def factor_kernel(spots, counts, k0, k1, live_at, take, s_ref, *refs):
    n_in = 2 * len(counts)
    ins = refs[:n_in]
    prev = refs[n_in : n_in + 5] if k0 else ()
    low_ref, lh_ref, ll_ref, wh_ref, wl_ref, a_s, l_s, d_s, w_s, u_s = refs[n_in + len(prev) :]
    live = s_ref[live_at]
    last = jnp.minimum(live, k1)
    first = 0
    for n, count in enumerate(counts):
        for t in range(count):
            r, c = spots[first + t]
            a_s[r * T : r * T + T, c * T : c * T + T] = ins[2 * n][t] + ins[2 * n + 1][t]
        first += count
    l_s[...] = jnp.zeros_like(l_s)
    ii = lax.broadcasted_iota(jnp.int32, (T, T), 0)
    jj = lax.broadcasted_iota(jnp.int32, (T, T), 1)
    eye = jnp.where(ii == jj, 1.0, 0.0).astype(f32)

    def dead(k, _):
        l_s[tl(k), tl(k)] = eye
        return 0

    lax.fori_loop(last, k1, dead, 0)
    tile_row = lax.broadcasted_iota(jnp.int32, (NP * T, T), 0) // T
    if k0:
        old = slice(0, k0 * T)
        for ref, src in zip((l_s, lh_ref, ll_ref), prev[:3]):
            ref[:, old] = src[...]
        for ref, src in zip((wh_ref, wl_ref), prev[3:]):
            ref[old, :] = src[...]

        def catch_up(j, _):
            xj = (prev[1][tl(j), :], prev[2][tl(j), :])
            a_s[:, tl(j)] = a_s[:, tl(j)] - dot3((prev[1][...], prev[2][...]), xj, NT)
            return 0

        lax.fori_loop(k0, last, catch_up, 0)

    def step(k, _):
        s = tl(k)
        d_s[...] = a_s[s, s]
        factor_tile(d_s, w_s, u_s)
        w = split(w_s[...])
        wh_ref[s, :] = w[0]
        wl_ref[s, :] = w[1]
        x = dot3(split(a_s[:, s]), w, NT)
        lh_ref[:, s], ll_ref[:, s] = split(x)
        l_s[:, s] = jnp.where((tile_row > k) & (tile_row < live), x, 0.0)
        l_s[s, s] = u_s[...].T

        def col(j, _):
            xj = (lh_ref[tl(j), s], ll_ref[tl(j), s])
            a_s[:, tl(j)] = a_s[:, tl(j)] - dot3((lh_ref[:, s], ll_ref[:, s]), xj, NT)
            return 0

        return lax.fori_loop(k + 1, last, col, 0)

    lax.fori_loop(k0, last, step, 0)
    if take is None:
        low_ref[...] = l_s[...]
    else:
        low_ref[...] = l_s[pl.ds(pl.multiple_of(take(s_ref), 64), low_ref.shape[0]), :]


def factor(scalars, pairs, spots, k0, k1, prev, live_at, take, rows):
    counts = tuple(x.shape[0] for x, _ in pairs)
    n = NP * T
    wide = k1 * T
    return call(
        functools.partial(factor_kernel, spots, counts, k0, k1, live_at, take),
        [scalars] + [x for pair in pairs for x in pair] + list(prev),
        [None] * (2 * len(pairs) + len(prev)),
        [shape(rows, wide), shape(n, wide, dtype=bf16), shape(n, wide, dtype=bf16)]
        + [shape(wide, T, dtype=bf16)] * 2,
        [pltpu.VMEM((n, wide), f32)] * 2 + [pltpu.VMEM((T, T), f32)] * 3,
        flops=20_000_000_000,
    )


def solve(x_ref, live, lh_ref, ll_ref, wh_ref, wl_ref, ph, plo):
    for k in range(NP):
        s = slice(k * T, k * T + T)

        @pl.when(k < live)
        def _():
            x = x_ref[:, s]
            if k:
                b = slice(0, k * T)
                x = x - dot3((ph[:, b], plo[:, b]), (lh_ref[s, b], ll_ref[s, b]), NT)
            x = dot3(split(x), (wh_ref[s, :], wl_ref[s, :]), NT)
            x_ref[:, s] = x
            xh, xl = split(x)
            ph[:, s] = xh
            plo[:, s] = xl

        @pl.when(k >= live)
        def _():
            x_ref[:, s] = jnp.zeros_like(x_ref[:, s])
            ph[:, s] = jnp.zeros_like(ph[:, s])
            plo[:, s] = jnp.zeros_like(plo[:, s])


def couple_one_kernel(s_ref, r_ref, c_ref, x_ref, inv):
    side = s_ref[SLO]
    invert(s_ref, OWN, NC, inv, 18)

    def tile(t, _):
        r = t // NP
        c = t % NP
        dst = (tl(r), tl(c))
        row = NP + side * 6 + r
        x_ref[dst] = r_ref[dst] * s_ref[FILL1 + t].astype(f32)

        @pl.when((inv[row] >= 0) & (inv[c] >= 0))
        def _():
            x_ref[dst] += c_ref[tl(inv[row]), tl(inv[c])]

        return 0

    lax.fori_loop(0, 36, tile, 0)


def panel_one_kernel(s_ref, x_ref, got_ref, lh, ll, wh, wl, p_ref, send_ref, ph, plo, inv2):
    side = s_ref[SLO]
    invert(s_ref, OTH, NC, inv2, 18)
    p_ref[...] = x_ref[...]

    def tile(t, count):
        r = t // NP
        c = t % NP
        row = NP + side * 6 + r
        hit = (inv2[row] >= 0) & (inv2[c] >= 0)

        @pl.when(hit)
        def _():
            p_ref[tl(r), tl(c)] += got_ref[count]

        return count + hit.astype(jnp.int32)

    lax.fori_loop(0, 36, tile, 0)
    solve(p_ref, s_ref[LIVE1], lh, ll, wh, wl, ph, plo)
    send_ref[...] = p_ref[:, pl.ds(pl.multiple_of((1 - side) * 384, T), 384)]


def own_kernel(s_ref, p_ref, t0_ref, t1_ref, own_ref, ph, plo):
    side = s_ref[SLO]
    ph[...], plo[...] = split(p_ref[...])
    for n in range(3):
        s = slice(n * 256, n * 256 + 256)
        base = jnp.where(side == 0, t0_ref[:, s], t1_ref[:, s])
        own_ref[:, s] = base - dot3((ph[...], plo[...]), (ph[s, :], plo[s, :]), NT)


def source_tile(side, inv, inv2, own_ref, cross_ref, c_ref, out_ref, at, r, c):
    i = inv2[r]
    j = inv2[c]
    used = (i >= 0) & (j >= 0)
    i = jnp.maximum(i, 0)
    j = jnp.maximum(j, 0)
    mi = (i // 6) == side
    mj = (j // 6) == side
    li = i % 6
    lj = j % 6

    @pl.when(used & mi & mj)
    def _():
        out_ref[at] = own_ref[tl(li), tl(lj)]

    @pl.when(used & mi & jnp.logical_not(mj))
    def _():
        out_ref[at] = cross_ref[tl(li), tl(lj)]

    @pl.when(used & jnp.logical_not(mi) & mj)
    def _():
        out_ref[at] = cross_ref[tl(lj), tl(li)].T

    @pl.when(jnp.logical_not(used) | (jnp.logical_not(mi) & jnp.logical_not(mj)))
    def _():
        out_ref[at] = jnp.zeros((T, T), f32)

    ci = inv[i + NP]
    cj = inv[j + NP]

    @pl.when(used & (ci >= 0) & (cj >= 0))
    def _():
        out_ref[at] += c_ref[tl(ci), tl(cj)]


def cross_kernel(
    s_ref, p_ref, q_ref, t1_ref, own_ref, c_ref, pv_ref, cross_ref, a_ref, b_ref, wide, inv, inv2
):
    side = s_ref[SLO]
    quarter = 2 * s_ref[SHI] + side
    mine = pl.ds(pl.multiple_of(side * 384, T), 384)
    pc = split(p_ref[:, mine])
    qh, ql = split(q_ref[...])
    for n in range(3):
        s = slice(n * 256, n * 256 + 256)
        base = jnp.where(side == 0, t1_ref[:, s], 0.0)
        cross_ref[:, s] = base - dot3(pc, (qh[s, :], ql[s, :]), NT)
    invert(s_ref, OWN, NC, inv, 18)
    invert(s_ref, MAP2, NU, inv2, 18)
    wide[...] = jnp.zeros_like(wide)
    wide[pl.ds(pl.multiple_of((quarter % 2) * 64, 64), 192), :] = pv_ref[...]
    base = (3 * quarter) // 2

    def emit(out_ref, first, row):
        def col(c, _):
            at = row * (row + 1) // 2 + c - first
            source_tile(side, inv, inv2, own_ref, cross_ref, c_ref, out_ref, at, row, c)

            @pl.when((row >= base) & (row < base + 2))
            def _():
                out_ref[at] += wide[tl(row - base), tl(c)]

            return 0

        lax.fori_loop(0, row + 1, col, 0)

    lax.fori_loop(0, 4, lambda r, _: (emit(a_ref, 0, r), 0)[1], 0)
    lax.fori_loop(4, 6, lambda r, _: (emit(b_ref, 10, r), 0)[1], 0)


def rows_two_kernel(first, width, s_ref, own_ref, cross_ref, c_ref, *refs):
    outs = refs[:4]
    inv, inv2 = refs[4:]
    lo = s_ref[SLO]
    hi = s_ref[SHI]
    invert(s_ref, OWN, NC, inv, 18)
    invert(s_ref, MAP2, NU, inv2, 18)
    half = width // 2
    orders = (
        (0, (1 - hi, 1 - lo), (1 - hi, lo)),
        (0, (hi, 1 - lo), (hi, lo)),
        (half, (1 - hi, 1 - lo), (hi, 1 - lo)),
        (half, (1 - hi, lo), (hi, lo)),
    )
    for out_ref, (skip, one, two) in zip(outs, orders):

        def tile(t, _):
            r = t // half
            later = (r >= 3).astype(jnp.int32)
            a = one[0] + (two[0] - one[0]) * later
            b = one[1] + (two[1] - one[1]) * later
            row = NP + 6 * a + 3 * b + r % 3
            col = first + skip + t % half
            source_tile(lo, inv, inv2, own_ref, cross_ref, c_ref, out_ref, t, row, col)
            return 0

        lax.fori_loop(0, 6 * half, tile, 0)


def rows_two(scalars, own, cross, block_c, first, width):
    count = 3 * width
    return call(
        functools.partial(rows_two_kernel, first, width),
        [scalars, own, cross, block_c],
        [None] * 3,
        [shape(count, T, T)] * 4,
        [pltpu.SMEM((18,), jnp.int32)] * 2,
    )


NINE = [(r, c) for r in range(3) for c in range(3)]
DX, DZ = [(0, 0), (1, 0), (1, 1)], [(2, 0), (2, 1), (2, 2)]
GX, GZ = NINE[:4], NINE[4:]


def chain_x(m, x, z, d):
    return (
        [(z, z, t) for t in DX]
        + [(z, x, t) for t in GX]
        + [(m, z, t) for t in NINE]
        + [(m, m, t) for t in DX]
        + [(m, d, t) for t in GX]
    )


def chain_z(m, x, z, d):
    return (
        [(x, x, t) for t in DZ]
        + [(x, z, t) for t in GZ]
        + [(m, x, t) for t in NINE]
        + [(m, m, t) for t in DZ]
        + [(m, d, t) for t in GZ]
    )


def trailing_two_kernel(
    s_ref, own_ref, cross_ref, c_ref, xs, xk, zs, zk, inv, inv2, rtab, ctab
):
    lo = s_ref[SLO]
    hi = s_ref[SHI]
    invert(s_ref, OWN, NC, inv, 18)
    invert(s_ref, MAP2, NU, inv2, 18)
    m, x, z, d = (
        NP + 3 * (2 * a + b) for a, b in ((hi, lo), (1 - hi, lo), (hi, 1 - lo), (1 - hi, 1 - lo))
    )
    for out_ref, tiles in (
        (xs, chain_x(x, m, d, z)),
        (xk, chain_x(m, x, z, d)),
        (zs, chain_z(z, d, m, x)),
        (zk, chain_z(m, x, z, d)),
    ):
        for n, (rq, cq, (r, c)) in enumerate(tiles):
            rtab[n] = rq + r
            ctab[n] = cq + c

        def tile(t, _):
            source_tile(lo, inv, inv2, own_ref, cross_ref, c_ref, out_ref, t, rtab[t], ctab[t])
            return 0

        lax.fori_loop(0, len(tiles), tile, 0)


def panel_two_kernel(
    s_ref, r_ref, xk, x1, x2, zk, z1, z2, lh, ll, wh, wl, p_ref, ph, plo
):
    for r in range(3):
        for c in range(3):
            t = 3 * r + c
            dst = (slice(r * T, r * T + T), slice(c * T, c * T + T))
            fill = s_ref[FILL2 + 6 * r + c].astype(f32)
            p_ref[dst] = r_ref[dst] * fill + ((xk[9 + t] + x1[9 + t]) + x2[t])
            dst = (dst[0], slice((c + 3) * T, (c + 4) * T))
            fill = s_ref[FILL2 + 6 * r + c + 3].astype(f32)
            p_ref[dst] = r_ref[dst] * fill + ((zk[9 + t] + z1[9 + t]) + z2[t])
    solve(p_ref, s_ref[LIVE2], lh, ll, wh, wl, ph, plo)


def schur_base_kernel(s_ref, r_ref, p_ref, xk, x1, x2, zk, z1, z2, out_ref):
    hi = s_ref[SHI]
    lo = s_ref[SLO]
    out_ref[...] = r_ref[:, NP * T :]
    m, x, z, d = (
        3 * (2 * a + b) for a, b in ((hi, lo), (1 - hi, lo), (hi, 1 - lo), (1 - hi, 1 - lo))
    )
    mine = split(p_ref[...])
    cols = pl.ds(pl.multiple_of(m * T, T), 384)
    out_ref[:, cols] = out_ref[:, cols] - dot3(mine, mine, NT)

    def add(quarter, r, c, value):
        out_ref[r * T : r * T + T, tl(quarter + c)] += value

    for k, r1, r2, diag, cross, pair in ((xk, x1, x2, DX, GX, z), (zk, z1, z2, DZ, GZ, x)):
        nd = len(diag)
        ng = len(cross)
        base = nd + ng + 9
        for n, (r, c) in enumerate(diag):
            v = (k[base + n] + r1[base + n]) + r2[n]
            add(m, r, c, v)
            if r != c:
                add(m, c, r, v.T)
        for n, (r, c) in enumerate(cross):
            v = (k[base + nd + n] + r1[base + nd + n]) + r2[nd + n]
            add(d, r, c, v)
        for n, (r, c) in enumerate(NINE):
            v = (k[nd + ng + n] + r1[nd + ng + n]) + r2[nd + ng + 3 * c + r].T
            add(pair, r, c, v)


def schur_kernel(s_ref, b_ref, p_ref, px, pz, pd0, pd1, out_ref):
    hi = s_ref[SHI]
    lo = s_ref[SLO]
    mine = split(p_ref[...])

    def minus(a, b, other):
        cols = pl.ds(pl.multiple_of((2 * a + b) * 384, T), 384)
        out_ref[:, cols] = b_ref[:, cols] - dot3(mine, split(other), NT)

    minus(1 - hi, lo, px[...])
    minus(hi, 1 - lo, pz[...])
    minus(1 - hi, 1 - lo, jnp.concatenate([pd0[...], pd1[...]], axis=0))
    cols = pl.ds(pl.multiple_of((2 * hi + lo) * 384, T), 384)
    out_ref[:, cols] = b_ref[:, cols]


def across(axis, values):
    size = lax.axis_size(axis)
    return lax.ppermute(values, axis, [(i, i ^ (size // 2)) for i in range(size)])


def program(
    contribution,
    pivot_one,
    rows_one,
    pivot_two,
    rows_two_in,
    map_one,
    map_two,
    fill_one,
    fill_two,
    live_one,
    live_two,
):
    size_lo = lax.axis_size("lo")
    size_hi = lax.axis_size("hi")
    half_lo = size_lo // 2
    half_hi = size_hi // 2
    lo = lax.axis_index("lo")
    hi = lax.axis_index("hi")
    side_lo = lo // half_lo
    side_hi = hi // half_hi
    front_lo = lo % half_lo
    front_hi = hi % half_hi
    quarter = 2 * side_hi + side_lo
    i32 = jnp.int32
    c = contribution[0, 0]
    rows1 = rows_one[0, 0]
    rows2 = rows_two_in[0, 0]
    smem = pltpu.SMEM((18,), i32)
    n = NP * T

    piv_a, piv_b, coup = call(
        functools.partial(gather_one_kernel, half_lo),
        [map_one[hi, lo], c, pivot_one[0, 0]],
        [None, None],
        [shape(11, T, T), shape(10, T, T), shape(16, T, T)],
        [smem],
    )
    piv_a, map_one, map_two, fill_one, fill_two, live_one, live_two = lax.optimization_barrier(
        (piv_a, map_one, map_two, fill_one, fill_two, live_one, live_two)
    )
    got_a = across("lo", piv_a)
    scalars = jnp.concatenate(
        [
            map_one[hi, lo],
            map_one[hi, (lo + half_lo) % size_lo],
            map_two[hi, front_lo],
            jnp.stack([side_lo, side_hi]).astype(i32),
            live_one[hi, front_lo][None],
            live_two[front_hi, front_lo][None],
            lax.dynamic_slice_in_dim(fill_one[hi, front_lo], side_lo * 6, 6, 0).reshape(36),
            lax.dynamic_slice_in_dim(fill_two[front_hi, front_lo], quarter * 3, 3, 0).reshape(18),
        ]
    )
    (x_one,) = call(
        couple_one_kernel, [scalars, rows1, c], [block(n, n, 0), None], [shape(n, n)], [smem]
    )
    piv_b, got_a = lax.optimization_barrier((piv_b, got_a))
    got_b = across("lo", piv_b)
    part = factor(scalars, [(piv_a, got_a)], BY_COL, 0, 2, (), LIVE1, None, n)
    coup, got_b = lax.optimization_barrier((coup, got_b))
    coup_got = across("lo", coup)
    lower_one, *fac1 = factor(
        scalars, [(piv_b, got_b)], BY_COL[11:], 2, NP, part, LIVE1, lambda s: s[SLO] * 384, 384
    )
    panel_one, send = call(
        panel_one_kernel,
        [scalars, x_one, coup_got, *fac1],
        [None] * 6,
        [shape(n, n), shape(n, n // 2)],
        [pltpu.VMEM((n, n), bf16)] * 2 + [smem],
        flops=3_000_000_000,
    )
    got = across("lo", send)
    (own,) = call(
        own_kernel,
        [scalars, panel_one, rows1, rows1],
        [None, block(n, n, 1), block(n, n, 2)],
        [shape(n, n)],
        [pltpu.VMEM((n, n), bf16)] * 2,
        flops=4_000_000_000,
    )
    cross, pa, pb = call(
        cross_kernel,
        [scalars, panel_one, got, rows1, own, c, pivot_two[0, 0]],
        [None, None, block(n, n, 2), None, None, None],
        [shape(n, n), shape(10, T, T), shape(11, T, T)],
        [pltpu.VMEM((2 * T, n), f32), smem, smem],
        flops=2_000_000_000,
    )
    pa1 = across("hi", pa)
    pb1 = across("lo", pb)
    pa, pb, cross = lax.optimization_barrier((pa, pb, cross))
    cxs, cxk, czs, czk = rows_two(scalars, own, cross, c, 0, NP)
    pa = pa + pa1
    pb = pb + pb1
    pa, pb, cxs, czs = lax.optimization_barrier((pa, pb, cxs, czs))
    pa2 = across("lo", pa)
    pb2 = across("hi", pb)
    cx1 = across("hi", cxs)
    cz1 = across("lo", czs)
    txs, txk, tzs, tzk = call(
        trailing_two_kernel,
        [scalars, own, cross, c],
        [None] * 3,
        [shape(23, T, T)] * 2 + [shape(25, T, T)] * 2,
        [smem, smem] + [pltpu.SMEM((32,), i32)] * 2,
    )
    tx1 = across("hi", txs)
    tz1 = across("lo", tzs)
    lower_two, *fac2 = factor(
        scalars,
        [(pa, pa2), (pb, pb2)],
        BY_ROW,
        0,
        NP,
        (),
        LIVE2,
        lambda s: (2 * s[SHI] + s[SLO]) * 192,
        192,
    )
    cx2 = across("lo", cxk[:9] + cx1[:9])
    cz2 = across("hi", czk[:9] + cz1[:9])
    tx = txk[:16] + tx1[:16]
    tz = tzk[:17] + tz1[:17]
    tx, tz, cx2, cz2 = lax.optimization_barrier((tx, tz, cx2, cz2))
    tx2 = across("lo", tx)
    tz2 = across("hi", tz)
    (panel_two,) = call(
        panel_two_kernel,
        [scalars, rows2, cxk, cx1, cx2, czk, cz1, cz2, *fac2],
        [block(384, n, 0)] + [None] * 10,
        [shape(384, n)],
        [pltpu.VMEM((384, n), bf16)] * 2,
        flops=2_000_000_000,
    )
    px = across("hi", panel_two)
    pz = across("lo", panel_two)
    pd0 = across("hi", pz[:192])
    pd1 = across("lo", px[192:])
    (base_two,) = call(
        schur_base_kernel,
        [scalars, rows2, panel_two, txk, tx1, tx2, tzk, tz1, tz2],
        [None] * 8,
        [shape(384, NU * T)],
        [],
        flops=1_000_000_000,
    )
    (schur_two,) = call(
        schur_kernel,
        [scalars, base_two, panel_two, px, pz, pd0, pd1],
        [None] * 6,
        [shape(384, NU * T)],
        [],
        flops=3_000_000_000,
    )
    return tuple(
        out[None, None] for out in (lower_one, panel_one, lower_two, panel_two, schur_two)
    )


def solution(mesh):
    split_spec = P("hi", "lo", None, None)
    return jax.shard_map(
        program,
        mesh=mesh,
        in_specs=(split_spec,) * 5 + (P(),) * 6,
        out_specs=(split_spec,) * 5,
        check_vma=False,
    )
```

```python
import functools
import jax
import jax.numpy as jnp
from jax import lax
from jax.experimental import pallas as pl
from jax.experimental.pallas import tpu as pltpu
from jax.sharding import PartitionSpec as P


T = 128
NP = 6
NU = 12
NC = 8
f32 = jnp.float32
bf16 = jnp.bfloat16
NT = ((1,), (1,))
OWN, OTH, MAP2, SLO, SHI, LIVE1, LIVE2, FILL1, FILL2 = 0, 8, 16, 28, 29, 30, 31, 32, 68


def tl(i):
    if isinstance(i, int):
        return slice(i * T, i * T + T)
    return pl.ds(pl.multiple_of(i * T, T), T)


def split(x):
    hi = x.astype(bf16)
    return hi, (x - hi.astype(f32)).astype(bf16)


def dot3(a, b, dims):
    (ah, al), (bh, bl) = a, b
    dn = (dims, ((), ()))
    f = lambda x, y: lax.dot_general(x, y, dn, preferred_element_type=f32)
    return f(ah, bh) + (f(ah, bl) + f(al, bh))


def call(kernel, args, specs, outs, scratch, flops=0, out_specs=None, aliases=None):
    whole = pl.BlockSpec(memory_space=pltpu.VMEM)
    in_specs = [whole if s is None else s for s in specs]
    nbytes = sum(4 * a.size for a in args[1:]) + sum(4 * o.size for o in outs)
    return pl.pallas_call(
        kernel,
        grid_spec=pltpu.PrefetchScalarGridSpec(
            num_scalar_prefetch=1,
            grid=(1,),
            in_specs=in_specs,
            out_specs=out_specs or [whole] * len(outs),
            scratch_shapes=scratch,
        ),
        out_shape=outs,
        input_output_aliases=aliases or {},
        compiler_params=pltpu.CompilerParams(vmem_limit_bytes=60 * 1024 * 1024),
        cost_estimate=pl.CostEstimate(flops=flops, bytes_accessed=nbytes, transcendentals=0),
    )(*args)


def shape(*dims, dtype=f32):
    return jax.ShapeDtypeStruct(dims, dtype)


def block(rows, cols, j):
    return pl.BlockSpec((rows, cols), lambda i, s: (0, j))


def invert(s_ref, first, count, inv_ref, size):
    for r in range(size):
        inv_ref[r] = -1
    for i in range(count):
        inv_ref[s_ref[first + i]] = i


def gather_tiles(side, inv, c_ref, p_ref, out_ref, first, last, skip):
    for c in range(first, last):
        base = BY_COL.index((c, c)) - skip - c

        def tile(r, _):
            at = base + r
            local = r - 3 * side

            @pl.when((local >= 0) & (local < 3))
            def _():
                out_ref[at] = p_ref[tl(local), tl(c)]

            @pl.when((local < 0) | (local >= 3))
            def _():
                out_ref[at] = jnp.zeros((T, T), f32)

            @pl.when((inv[r] >= 0) & (inv[c] >= 0))
            def _():
                out_ref[at] += c_ref[tl(inv[r]), tl(inv[c])]

            return 0

        lax.fori_loop(c, NP, tile, 0)


def gather_a_kernel(half_lo, s_ref, c_ref, p_ref, a_ref, inv):
    side = lax.axis_index("lo") // half_lo
    invert(s_ref, OWN, NC, inv, 18)
    gather_tiles(side, inv, c_ref, p_ref, a_ref, 0, 2, 0)


def gather_b_kernel(half_lo, s_ref, c_ref, p_ref, b_ref, coup_ref, inv):
    side = lax.axis_index("lo") // half_lo
    invert(s_ref, OWN, NC, inv, 18)
    gather_tiles(side, inv, c_ref, p_ref, b_ref, 2, NP, 11)

    def coup_tile(t, count):
        row = inv[NP + (1 - side) * 6 + t // NP]
        col = inv[t % NP]
        hit = (row >= 0) & (col >= 0)

        @pl.when(hit)
        def _():
            coup_ref[count] = c_ref[tl(row), tl(col)]

        return count + hit.astype(jnp.int32)

    lax.fori_loop(0, 36, coup_tile, 0)


def factor_tile(x_ref, w_ref, u_ref):
    lane = lax.broadcasted_iota(jnp.int32, (8, T), 1)
    wide = lambda v: jnp.broadcast_to(v, (8, T))
    cols = lambda x, r0: [wide(x[:, r0 + k : r0 + k + 1]) for k in range(8)]
    diag = cols(x_ref[0:8, :], 0)
    x = x_ref[8:16, :]
    ahead = (cols(x, 0), cols(x, 8))
    for g in range(16):
        r0 = 8 * g
        inside = (lane >= r0) & (lane < r0 + 8)
        e = [[wide(diag[k][i : i + 1, :]) for k in range(i + 1)] for i in range(8)]
        l = [[None] * 8 for _ in range(8)]
        rinv = [None] * 8
        for j in range(8):
            rinv[j] = lax.rsqrt(e[j][j])
            l[j][j] = e[j][j] * rinv[j]
            for i in range(j + 1, 8):
                l[i][j] = e[i][j] * rinv[j]
            for i in range(j + 1, 8):
                for k in range(j + 1, i + 1):
                    e[i][k] = e[i][k] - l[i][j] * l[k][j]

        def eliminate(c):
            for j in range(8):
                a = c[j]
                for k in range(j):
                    a = a - l[j][k] * c[k]
                c[j] = a * rinv[j]
            return c

        if g < 15:
            c1 = eliminate(ahead[0])
            diag = ahead[1]
            for j in range(8):
                for k in range(8):
                    diag[k] = diag[k] - c1[j] * wide(c1[j][k : k + 1, :])
        z = [None] * 8
        for j in range(8):
            row = wide(x_ref[r0 + j : r0 + j + 1, :])
            a = jnp.where(inside, jnp.where(lane == r0 + j, 1.0, 0.0), row)
            for k in range(j):
                a = a - l[j][k] * z[k]
            z[j] = a * rinv[j]
            d = jnp.where(lane < r0, 0.0, z[j])
            for k in range(j, 8):
                d = jnp.where(lane == r0 + k, l[k][j], d)
            if j:
                d = jnp.where(lane < r0 + j, 0.0, d)
            u_ref[r0 + j : r0 + j + 1, :] = d[:1]
            w_ref[r0 + j : r0 + j + 1, :] = jnp.where(lane < r0 + 8, z[j], 0.0)[:1]
        y = [None] * 8
        for j in reversed(range(8)):
            a = z[j]
            for i in range(j + 1, 8):
                a = a - l[i][j] * y[i]
            y[j] = a * rinv[j]
        for r in range(g + 1, 16):
            q = 8 * r
            x = x_ref[q : q + 8, :]
            if r == g + 1:
                c, v = c1, z
            else:
                c, v = cols(x, r0), y
            x = jnp.where(inside, 0.0, x)
            for j in range(8):
                x = x - c[j] * v[j]
            x_ref[q : q + 8, :] = x
            if r == g + 2:
                ahead = (cols(x, r0 + 8), cols(x, r0 + 16))


BY_ROW = [(r, c) for r in range(NP) for c in range(r + 1)]
BY_COL = [(r, c) for c in range(NP) for r in range(c, NP)]


def factor_kernel(spots, counts, k0, k1, live_at, take, s_ref, *refs):
    n_in = 2 * len(counts)
    ins = refs[:n_in]
    prev = refs[n_in : n_in + 5] if k0 else ()
    low_ref, lh_ref, ll_ref, wh_ref, wl_ref, a_s, l_s, d_s, w_s, u_s = refs[n_in + len(prev) :]
    live = s_ref[live_at]
    last = jnp.minimum(live, k1)
    first = 0
    for n, count in enumerate(counts):
        for t in range(count):
            r, c = spots[first + t]
            a_s[r * T : r * T + T, c * T : c * T + T] = ins[2 * n][t] + ins[2 * n + 1][t]
        first += count
    l_s[...] = jnp.zeros_like(l_s)
    ii = lax.broadcasted_iota(jnp.int32, (T, T), 0)
    jj = lax.broadcasted_iota(jnp.int32, (T, T), 1)
    eye = jnp.where(ii == jj, 1.0, 0.0).astype(f32)

    def dead(k, _):
        l_s[tl(k), tl(k)] = eye
        return 0

    lax.fori_loop(last, k1, dead, 0)
    tile_row = lax.broadcasted_iota(jnp.int32, (NP * T, T), 0) // T
    if k0:
        old = slice(0, k0 * T)
        for ref, src in zip((l_s, lh_ref, ll_ref), prev[:3]):
            ref[:, old] = src[...]
        for ref, src in zip((wh_ref, wl_ref), prev[3:]):
            ref[old, :] = src[...]

        def catch_up(j, _):
            xj = (prev[1][tl(j), :], prev[2][tl(j), :])
            a_s[:, tl(j)] = a_s[:, tl(j)] - dot3((prev[1][...], prev[2][...]), xj, NT)
            return 0

        lax.fori_loop(k0, last, catch_up, 0)

    def step(k, _):
        s = tl(k)
        d_s[...] = a_s[s, s]
        factor_tile(d_s, w_s, u_s)
        w = split(w_s[...])
        wh_ref[s, :] = w[0]
        wl_ref[s, :] = w[1]
        x = dot3(split(a_s[:, s]), w, NT)
        lh_ref[:, s], ll_ref[:, s] = split(x)
        l_s[:, s] = jnp.where((tile_row > k) & (tile_row < live), x, 0.0)
        l_s[s, s] = u_s[...].T

        def col(j, _):
            xj = (lh_ref[tl(j), s], ll_ref[tl(j), s])
            a_s[:, tl(j)] = a_s[:, tl(j)] - dot3((lh_ref[:, s], ll_ref[:, s]), xj, NT)
            return 0

        return lax.fori_loop(k + 1, last, col, 0)

    lax.fori_loop(k0, last, step, 0)
    if take is None:
        low_ref[...] = l_s[...]
    else:
        low_ref[...] = l_s[pl.ds(pl.multiple_of(take(s_ref), 64), low_ref.shape[0]), :]


def factor(scalars, pairs, spots, k0, k1, prev, live_at, take, rows):
    counts = tuple(x.shape[0] for x, _ in pairs)
    n = NP * T
    wide = k1 * T
    return call(
        functools.partial(factor_kernel, spots, counts, k0, k1, live_at, take),
        [scalars] + [x for pair in pairs for x in pair] + list(prev),
        [None] * (2 * len(pairs) + len(prev)),
        [shape(rows, wide), shape(n, wide, dtype=bf16), shape(n, wide, dtype=bf16)]
        + [shape(wide, T, dtype=bf16)] * 2,
        [pltpu.VMEM((n, wide), f32)] * 2 + [pltpu.VMEM((T, T), f32)] * 3,
        flops=20_000_000_000,
    )


def solve(x_ref, live, lh_ref, ll_ref, wh_ref, wl_ref, ph, plo):
    for k in range(NP):
        s = slice(k * T, k * T + T)

        @pl.when(k < live)
        def _():
            x = x_ref[:, s]
            if k:
                b = slice(0, k * T)
                x = x - dot3((ph[:, b], plo[:, b]), (lh_ref[s, b], ll_ref[s, b]), NT)
            x = dot3(split(x), (wh_ref[s, :], wl_ref[s, :]), NT)
            x_ref[:, s] = x
            xh, xl = split(x)
            ph[:, s] = xh
            plo[:, s] = xl

        @pl.when(k >= live)
        def _():
            x_ref[:, s] = jnp.zeros_like(x_ref[:, s])
            ph[:, s] = jnp.zeros_like(ph[:, s])
            plo[:, s] = jnp.zeros_like(plo[:, s])


def couple_one_kernel(s_ref, r_ref, c_ref, x_ref, inv):
    side = s_ref[SLO]
    invert(s_ref, OWN, NC, inv, 18)

    def tile(t, _):
        r = t // NP
        c = t % NP
        dst = (tl(r), tl(c))
        row = NP + side * 6 + r
        x_ref[dst] = r_ref[dst] * s_ref[FILL1 + t].astype(f32)

        @pl.when((inv[row] >= 0) & (inv[c] >= 0))
        def _():
            x_ref[dst] += c_ref[tl(inv[row]), tl(inv[c])]

        return 0

    lax.fori_loop(0, 36, tile, 0)


def panel_one_kernel(s_ref, x_ref, got_ref, lh, ll, wh, wl, p_ref, send_ref, ph, plo, inv2):
    side = s_ref[SLO]
    invert(s_ref, OTH, NC, inv2, 18)
    p_ref[...] = x_ref[...]

    def tile(t, count):
        r = t // NP
        c = t % NP
        row = NP + side * 6 + r
        hit = (inv2[row] >= 0) & (inv2[c] >= 0)

        @pl.when(hit)
        def _():
            p_ref[tl(r), tl(c)] += got_ref[count]

        return count + hit.astype(jnp.int32)

    lax.fori_loop(0, 36, tile, 0)
    solve(p_ref, s_ref[LIVE1], lh, ll, wh, wl, ph, plo)
    send_ref[...] = p_ref[:, pl.ds(pl.multiple_of((1 - side) * 384, T), 384)]


def own_kernel(
    s_ref, p_ref, t0_ref, t1_ref, c_ref, pv_ref, own_ref, piv_ref, ph, plo, wide, inv, inv2
):
    side = s_ref[SLO]
    quarter = 2 * s_ref[SHI] + side
    ph[...], plo[...] = split(p_ref[...])
    for n in range(3):
        s = slice(n * 256, n * 256 + 256)
        base = jnp.where(side == 0, t0_ref[:, s], t1_ref[:, s])
        own_ref[:, s] = base - dot3((ph[...], plo[...]), (ph[s, :], plo[s, :]), NT)
    invert(s_ref, OWN, NC, inv, 18)
    invert(s_ref, MAP2, NU, inv2, 18)
    wide[...] = jnp.zeros_like(wide)
    wide[pl.ds(pl.multiple_of((quarter % 2) * 64, 64), 192), :] = pv_ref[...]
    base = (3 * quarter) // 2

    def emit(row, _):
        def col(c, _):
            at = row * (row + 1) // 2 + c
            source_tile(side, inv, inv2, own_ref, None, c_ref, piv_ref, at, row, c)

            @pl.when((row >= base) & (row < base + 2))
            def _():
                piv_ref[at] += wide[tl(row - base), tl(c)]

            return 0

        return lax.fori_loop(0, row + 1, col, 0)

    lax.fori_loop(0, NP, emit, 0)


def source_tile(side, inv, inv2, own_ref, cross_ref, c_ref, out_ref, at, r, c):
    i = inv2[r]
    j = inv2[c]
    used = (i >= 0) & (j >= 0)
    i = jnp.maximum(i, 0)
    j = jnp.maximum(j, 0)
    mi = (i // 6) == side
    mj = (j // 6) == side
    li = i % 6
    lj = j % 6

    @pl.when(used & mi & mj)
    def _():
        out_ref[at] = own_ref[tl(li), tl(lj)]

    if cross_ref is None:
        empty = jnp.logical_not(used & mi & mj)
    else:
        empty = jnp.logical_not(used) | (jnp.logical_not(mi) & jnp.logical_not(mj))

        @pl.when(used & mi & jnp.logical_not(mj))
        def _():
            out_ref[at] = cross_ref[tl(li), tl(lj)]

        @pl.when(used & jnp.logical_not(mi) & mj)
        def _():
            out_ref[at] = cross_ref[tl(lj), tl(li)].T

    @pl.when(empty)
    def _():
        out_ref[at] = jnp.zeros((T, T), f32)

    ci = inv[i + NP]
    cj = inv[j + NP]

    @pl.when(used & (ci >= 0) & (cj >= 0))
    def _():
        out_ref[at] += c_ref[tl(ci), tl(cj)]


def cross_kernel(s_ref, p_ref, q_ref, t1_ref, piv_ref, cross_ref, a_ref, b_ref, inv2):
    side = s_ref[SLO]
    pc = split(p_ref[...])
    qh, ql = split(q_ref[...])
    for n in range(3):
        s = slice(n * 256, n * 256 + 256)
        base = jnp.where(side == 0, t1_ref[:, s], 0.0)
        cross_ref[:, s] = base - dot3(pc, (qh[s, :], ql[s, :]), NT)
    invert(s_ref, MAP2, NU, inv2, 18)
    a_ref[...] = piv_ref[0:10]
    b_ref[...] = piv_ref[10:21]

    def emit(out_ref, first, row):
        def col(c, _):
            at = row * (row + 1) // 2 + c - first
            i = inv2[row]
            j = inv2[c]
            used = (i >= 0) & (j >= 0)
            i = jnp.maximum(i, 0)
            j = jnp.maximum(j, 0)
            mi = (i // 6) == side
            mj = (j // 6) == side

            @pl.when(used & mi & jnp.logical_not(mj))
            def _():
                out_ref[at] += cross_ref[tl(i % 6), tl(j % 6)]

            @pl.when(used & jnp.logical_not(mi) & mj)
            def _():
                out_ref[at] += cross_ref[tl(j % 6), tl(i % 6)].T

            return 0

        lax.fori_loop(0, row + 1, col, 0)

    lax.fori_loop(0, 4, lambda r, _: (emit(a_ref, 0, r), 0)[1], 0)
    lax.fori_loop(4, 6, lambda r, _: (emit(b_ref, 10, r), 0)[1], 0)


def rows_two_kernel(first, width, s_ref, own_ref, cross_ref, c_ref, *refs):
    outs = refs[:4]
    inv, inv2 = refs[4:]
    lo = s_ref[SLO]
    hi = s_ref[SHI]
    invert(s_ref, OWN, NC, inv, 18)
    invert(s_ref, MAP2, NU, inv2, 18)
    half = width // 2
    orders = (
        (0, (1 - hi, 1 - lo), (1 - hi, lo)),
        (0, (hi, 1 - lo), (hi, lo)),
        (half, (1 - hi, 1 - lo), (hi, 1 - lo)),
        (half, (1 - hi, lo), (hi, lo)),
    )
    for out_ref, (skip, one, two) in zip(outs, orders):

        def tile(t, _):
            r = t // half
            later = (r >= 3).astype(jnp.int32)
            a = one[0] + (two[0] - one[0]) * later
            b = one[1] + (two[1] - one[1]) * later
            row = NP + 6 * a + 3 * b + r % 3
            col = first + skip + t % half
            source_tile(lo, inv, inv2, own_ref, cross_ref, c_ref, out_ref, t, row, col)
            return 0

        lax.fori_loop(0, 6 * half, tile, 0)


def rows_two(scalars, own, cross, block_c, first, width):
    count = 3 * width
    return call(
        functools.partial(rows_two_kernel, first, width),
        [scalars, own, cross, block_c],
        [None] * 3,
        [shape(count, T, T)] * 4,
        [pltpu.SMEM((18,), jnp.int32)] * 2,
    )


NINE = [(r, c) for r in range(3) for c in range(3)]
DX, DZ = [(0, 0), (1, 0), (1, 1)], [(2, 0), (2, 1), (2, 2)]
GX, GZ = NINE[:4], NINE[4:]


def chain_x(m, x, z, d):
    return (
        [(z, z, t) for t in DX]
        + [(z, x, t) for t in GX]
        + [(m, z, t) for t in NINE]
        + [(m, m, t) for t in DX]
        + [(m, d, t) for t in GX]
    )


def chain_z(m, x, z, d):
    return (
        [(x, x, t) for t in DZ]
        + [(x, z, t) for t in GZ]
        + [(m, x, t) for t in NINE]
        + [(m, m, t) for t in DZ]
        + [(m, d, t) for t in GZ]
    )


def trailing_two_kernel(
    s_ref, own_ref, cross_ref, c_ref, xs, xk, zs, zk, inv, inv2, rtab, ctab
):
    lo = s_ref[SLO]
    hi = s_ref[SHI]
    invert(s_ref, OWN, NC, inv, 18)
    invert(s_ref, MAP2, NU, inv2, 18)
    m, x, z, d = (
        NP + 3 * (2 * a + b) for a, b in ((hi, lo), (1 - hi, lo), (hi, 1 - lo), (1 - hi, 1 - lo))
    )
    for out_ref, tiles in (
        (xs, chain_x(x, m, d, z)),
        (xk, chain_x(m, x, z, d)),
        (zs, chain_z(z, d, m, x)),
        (zk, chain_z(m, x, z, d)),
    ):
        for n, (rq, cq, (r, c)) in enumerate(tiles):
            rtab[n] = rq + r
            ctab[n] = cq + c

        def tile(t, _):
            source_tile(lo, inv, inv2, own_ref, cross_ref, c_ref, out_ref, t, rtab[t], ctab[t])
            return 0

        lax.fori_loop(0, len(tiles), tile, 0)


def panel_two_kernel(
    s_ref, r_ref, xk, x1, x2, zk, z1, z2, lh, ll, wh, wl, p_ref, ph, plo
):
    for r in range(3):
        for c in range(3):
            t = 3 * r + c
            dst = (slice(r * T, r * T + T), slice(c * T, c * T + T))
            fill = s_ref[FILL2 + 6 * r + c].astype(f32)
            p_ref[dst] = r_ref[dst] * fill + ((xk[9 + t] + x1[9 + t]) + x2[t])
            dst = (dst[0], slice((c + 3) * T, (c + 4) * T))
            fill = s_ref[FILL2 + 6 * r + c + 3].astype(f32)
            p_ref[dst] = r_ref[dst] * fill + ((zk[9 + t] + z1[9 + t]) + z2[t])
    solve(p_ref, s_ref[LIVE2], lh, ll, wh, wl, ph, plo)


def schur_base_kernel(s_ref, r_ref, p_ref, xk, x1, x2, zk, z1, z2, out_ref):
    hi = s_ref[SHI]
    lo = s_ref[SLO]
    out_ref[...] = r_ref[:, NP * T :]
    m, x, z, d = (
        3 * (2 * a + b) for a, b in ((hi, lo), (1 - hi, lo), (hi, 1 - lo), (1 - hi, 1 - lo))
    )
    mine = split(p_ref[...])
    cols = pl.ds(pl.multiple_of(m * T, T), 384)
    out_ref[:, cols] = out_ref[:, cols] - dot3(mine, mine, NT)

    def add(quarter, r, c, value):
        out_ref[r * T : r * T + T, tl(quarter + c)] += value

    for k, r1, r2, diag, cross, pair in ((xk, x1, x2, DX, GX, z), (zk, z1, z2, DZ, GZ, x)):
        nd = len(diag)
        ng = len(cross)
        base = nd + ng + 9
        for n, (r, c) in enumerate(diag):
            v = (k[base + n] + r1[base + n]) + r2[n]
            add(m, r, c, v)
            if r != c:
                add(m, c, r, v.T)
        for n, (r, c) in enumerate(cross):
            v = (k[base + nd + n] + r1[base + nd + n]) + r2[nd + n]
            add(d, r, c, v)
        for n, (r, c) in enumerate(NINE):
            v = (k[nd + ng + n] + r1[nd + ng + n]) + r2[nd + ng + 3 * c + r].T
            add(pair, r, c, v)


def schur_near_kernel(s_ref, b_ref, p_ref, px, pz, out_ref):
    hi = s_ref[SHI]
    lo = s_ref[SLO]
    mine = split(p_ref[...])
    out_ref[...] = b_ref[...]
    for a, b, other in ((1 - hi, lo, px), (hi, 1 - lo, pz)):
        cols = pl.ds(pl.multiple_of((2 * a + b) * 384, T), 384)
        out_ref[:, cols] = b_ref[:, cols] - dot3(mine, split(other[...]), NT)


def schur_far_kernel(s_ref, b_ref, p_ref, pd0, pd1, out_ref):
    other = split(jnp.concatenate([pd0[...], pd1[...]], axis=0))
    out_ref[...] = b_ref[...] - dot3(split(p_ref[...]), other, NT)


def across(axis, values):
    size = lax.axis_size(axis)
    return lax.ppermute(values, axis, [(i, i ^ (size // 2)) for i in range(size)])


def program(
    contribution,
    pivot_one,
    rows_one,
    pivot_two,
    rows_two_in,
    map_one,
    map_two,
    fill_one,
    fill_two,
    live_one,
    live_two,
):
    size_lo = lax.axis_size("lo")
    size_hi = lax.axis_size("hi")
    half_lo = size_lo // 2
    half_hi = size_hi // 2
    lo = lax.axis_index("lo")
    hi = lax.axis_index("hi")
    side_lo = lo // half_lo
    side_hi = hi // half_hi
    front_lo = lo % half_lo
    front_hi = hi % half_hi
    quarter = 2 * side_hi + side_lo
    i32 = jnp.int32
    c = contribution[0, 0]
    rows1 = rows_one[0, 0]
    rows2 = rows_two_in[0, 0]
    smem = pltpu.SMEM((18,), i32)
    n = NP * T

    own_map = map_one[hi, lo]
    (piv_a,) = call(
        functools.partial(gather_a_kernel, half_lo),
        [own_map, c, pivot_one[0, 0]],
        [None, block(384, 256, 0)],
        [shape(11, T, T)],
        [smem],
    )
    piv_a, map_one, map_two, fill_one, fill_two, live_one, live_two, own_map = (
        lax.optimization_barrier(
            (piv_a, map_one, map_two, fill_one, fill_two, live_one, live_two, own_map)
        )
    )
    got_a = across("lo", piv_a)
    piv_b, coup = call(
        functools.partial(gather_b_kernel, half_lo),
        [own_map, c, pivot_one[0, 0]],
        [None, None],
        [shape(10, T, T), shape(16, T, T)],
        [smem],
    )
    scalars = jnp.concatenate(
        [
            map_one[hi, lo],
            map_one[hi, (lo + half_lo) % size_lo],
            map_two[hi, front_lo],
            jnp.stack([side_lo, side_hi]).astype(i32),
            live_one[hi, front_lo][None],
            live_two[front_hi, front_lo][None],
            lax.dynamic_slice_in_dim(fill_one[hi, front_lo], side_lo * 6, 6, 0).reshape(36),
            lax.dynamic_slice_in_dim(fill_two[front_hi, front_lo], quarter * 3, 3, 0).reshape(18),
        ]
    )
    (x_one,) = call(
        couple_one_kernel, [scalars, rows1, c], [block(n, n, 0), None], [shape(n, n)], [smem]
    )
    piv_b, got_a = lax.optimization_barrier((piv_b, got_a))
    got_b = across("lo", piv_b)
    part = factor(scalars, [(piv_a, got_a)], BY_COL, 0, 2, (), LIVE1, None, n)
    coup, got_b = lax.optimization_barrier((coup, got_b))
    coup_got = across("lo", coup)
    lower_one, *fac1 = factor(
        scalars, [(piv_b, got_b)], BY_COL[11:], 2, NP, part, LIVE1, lambda s: s[SLO] * 384, 384
    )
    panel_one, send = call(
        panel_one_kernel,
        [scalars, x_one, coup_got, *fac1],
        [None] * 6,
        [shape(n, n), shape(n, n // 2)],
        [pltpu.VMEM((n, n), bf16)] * 2 + [smem],
        flops=3_000_000_000,
    )
    got = across("lo", send)
    own, piv = call(
        own_kernel,
        [scalars, panel_one, rows1, rows1, c, pivot_two[0, 0]],
        [None, block(n, n, 1), block(n, n, 2), None, None],
        [shape(n, n), shape(21, T, T)],
        [pltpu.VMEM((n, n), bf16)] * 2 + [pltpu.VMEM((2 * T, n), f32), smem, smem],
        flops=4_000_000_000,
    )
    cross, pa, pb = call(
        cross_kernel,
        [scalars, panel_one, got, rows1, piv],
        [pl.BlockSpec((n, n // 2), lambda i, s: (0, s[SLO])), None, block(n, n, 2), None],
        [shape(n, n), shape(10, T, T), shape(11, T, T)],
        [smem],
        flops=2_000_000_000,
    )
    pa1 = across("hi", pa)
    pb1 = across("lo", pb)
    pa, pb, cross = lax.optimization_barrier((pa, pb, cross))
    cxs, cxk, czs, czk = rows_two(scalars, own, cross, c, 0, NP)
    pa = pa + pa1
    pb = pb + pb1
    pa, pb, cxs, czs = lax.optimization_barrier((pa, pb, cxs, czs))
    pa2 = across("lo", pa)
    pb2 = across("hi", pb)
    cx1 = across("hi", cxs)
    cz1 = across("lo", czs)
    txs, txk, tzs, tzk = call(
        trailing_two_kernel,
        [scalars, own, cross, c],
        [None] * 3,
        [shape(23, T, T)] * 2 + [shape(25, T, T)] * 2,
        [smem, smem] + [pltpu.SMEM((32,), i32)] * 2,
    )
    tx1 = across("hi", txs)
    tz1 = across("lo", tzs)
    lower_two, *fac2 = factor(
        scalars,
        [(pa, pa2), (pb, pb2)],
        BY_ROW,
        0,
        NP,
        (),
        LIVE2,
        lambda s: (2 * s[SHI] + s[SLO]) * 192,
        192,
    )
    cx2 = across("lo", cxk[:9] + cx1[:9])
    cz2 = across("hi", czk[:9] + cz1[:9])
    tx = txk[:16] + tx1[:16]
    tz = tzk[:17] + tz1[:17]
    tx, tz, cx2, cz2 = lax.optimization_barrier((tx, tz, cx2, cz2))
    tx2 = across("lo", tx)
    tz2 = across("hi", tz)
    (panel_two,) = call(
        panel_two_kernel,
        [scalars, rows2, cxk, cx1, cx2, czk, cz1, cz2, *fac2],
        [block(384, n, 0)] + [None] * 10,
        [shape(384, n)],
        [pltpu.VMEM((384, n), bf16)] * 2,
        flops=2_000_000_000,
    )
    px = across("hi", panel_two)
    pz = across("lo", panel_two)
    pd0 = across("hi", pz[:192])
    pd1 = across("lo", px[192:])
    (base_two,) = call(
        schur_base_kernel,
        [scalars, rows2, panel_two, txk, tx1, tx2, tzk, tz1, tz2],
        [None] * 8,
        [shape(384, NU * T)],
        [],
        flops=1_000_000_000,
    )
    (near_two,) = call(
        schur_near_kernel,
        [scalars, base_two, panel_two, px, pz],
        [None] * 4,
        [shape(384, NU * T)],
        [],
        flops=2_000_000_000,
    )
    far = pl.BlockSpec((384, 384), lambda i, s: (0, 2 * (1 - s[SHI]) + 1 - s[SLO]))
    (schur_two,) = call(
        schur_far_kernel,
        [scalars, near_two, panel_two, pd0, pd1],
        [far, None, None, None],
        [shape(384, NU * T)],
        [],
        flops=1_000_000_000,
        out_specs=[far],
        aliases={1: 0},
    )
    return tuple(
        out[None, None] for out in (lower_one, panel_one, lower_two, panel_two, schur_two)
    )


def solution(mesh):
    split_spec = P("hi", "lo", None, None)
    return jax.shard_map(
        program,
        mesh=mesh,
        in_specs=(split_spec,) * 5 + (P(),) * 6,
        out_specs=(split_spec,) * 5,
        check_vma=False,
    )
```

```python
import functools
import jax
import jax.numpy as jnp
from jax import lax
from jax.experimental import pallas as pl
from jax.experimental.pallas import tpu as pltpu
from jax.sharding import PartitionSpec as P


T = 128
NP = 6
NU = 12
NC = 8
f32 = jnp.float32
bf16 = jnp.bfloat16
NN = ((1,), (0,))
NT = ((1,), (1,))
OWN, OTH, MAP2, SLO, SHI, LIVE1, LIVE2, FILL1, FILL2 = 0, 8, 16, 28, 29, 30, 31, 32, 68


def tl(i):
    if isinstance(i, int):
        return slice(i * T, i * T + T)
    return pl.ds(pl.multiple_of(i * T, T), T)


def split(x):
    hi = x.astype(bf16)
    return hi, (x - hi.astype(f32)).astype(bf16)


def dot3(a, b, dims):
    (ah, al), (bh, bl) = a, b
    dn = (dims, ((), ()))
    f = lambda x, y: lax.dot_general(x, y, dn, preferred_element_type=f32)
    return f(ah, bh) + (f(ah, bl) + f(al, bh))


def call(kernel, args, specs, outs, scratch, flops=0, out_specs=None, aliases=None):
    whole = pl.BlockSpec(memory_space=pltpu.VMEM)
    in_specs = [whole if s is None else s for s in specs]
    nbytes = sum(4 * a.size for a in args[1:]) + sum(4 * o.size for o in outs)
    return pl.pallas_call(
        kernel,
        grid_spec=pltpu.PrefetchScalarGridSpec(
            num_scalar_prefetch=1,
            grid=(1,),
            in_specs=in_specs,
            out_specs=out_specs or [whole] * len(outs),
            scratch_shapes=scratch,
        ),
        out_shape=outs,
        input_output_aliases=aliases or {},
        compiler_params=pltpu.CompilerParams(vmem_limit_bytes=60 * 1024 * 1024),
        cost_estimate=pl.CostEstimate(flops=flops, bytes_accessed=nbytes, transcendentals=0),
    )(*args)


def shape(*dims, dtype=f32):
    return jax.ShapeDtypeStruct(dims, dtype)


def block(rows, cols, j):
    return pl.BlockSpec((rows, cols), lambda i, s: (0, j))


def invert(s_ref, first, count, inv_ref, size):
    for r in range(size):
        inv_ref[r] = -1
    for i in range(count):
        inv_ref[s_ref[first + i]] = i


def gather_tiles(side, inv, c_ref, p_ref, out_ref, first, last, skip):
    for c in range(first, last):
        base = BY_COL.index((c, c)) - skip - c

        def tile(r, _):
            at = base + r
            local = r - 3 * side

            @pl.when((local >= 0) & (local < 3))
            def _():
                out_ref[at] = p_ref[tl(local), tl(c)]

            @pl.when((local < 0) | (local >= 3))
            def _():
                out_ref[at] = jnp.zeros((T, T), f32)

            @pl.when((inv[r] >= 0) & (inv[c] >= 0))
            def _():
                out_ref[at] += c_ref[tl(inv[r]), tl(inv[c])]

            return 0

        lax.fori_loop(c, NP, tile, 0)


def gather_a_kernel(half_lo, s_ref, c_ref, p_ref, a_ref, inv):
    side = lax.axis_index("lo") // half_lo
    invert(s_ref, OWN, NC, inv, 18)
    gather_tiles(side, inv, c_ref, p_ref, a_ref, 0, 2, 0)


def gather_b_kernel(half_lo, s_ref, c_ref, p_ref, b_ref, coup_ref, inv):
    side = lax.axis_index("lo") // half_lo
    invert(s_ref, OWN, NC, inv, 18)
    gather_tiles(side, inv, c_ref, p_ref, b_ref, 2, NP, 11)

    def coup_tile(t, count):
        row = inv[NP + (1 - side) * 6 + t // NP]
        col = inv[t % NP]
        hit = (row >= 0) & (col >= 0)

        @pl.when(hit)
        def _():
            coup_ref[count] = c_ref[tl(row), tl(col)]

        return count + hit.astype(jnp.int32)

    lax.fori_loop(0, 36, coup_tile, 0)


def factor_tile(x_ref, w_ref, u_ref):
    lane = lax.broadcasted_iota(jnp.int32, (8, T), 1)
    wide = lambda v: jnp.broadcast_to(v, (8, T))
    cols = lambda x, r0: [wide(x[:, r0 + k : r0 + k + 1]) for k in range(8)]
    diag = cols(x_ref[0:8, :], 0)
    x = x_ref[8:16, :]
    ahead = (cols(x, 0), cols(x, 8))
    for g in range(16):
        r0 = 8 * g
        inside = (lane >= r0) & (lane < r0 + 8)
        e = [[wide(diag[k][i : i + 1, :]) for k in range(i + 1)] for i in range(8)]
        l = [[None] * 8 for _ in range(8)]
        rinv = [None] * 8
        for j in range(8):
            rinv[j] = lax.rsqrt(e[j][j])
            l[j][j] = e[j][j] * rinv[j]
            for i in range(j + 1, 8):
                l[i][j] = e[i][j] * rinv[j]
            for i in range(j + 1, 8):
                for k in range(j + 1, i + 1):
                    e[i][k] = e[i][k] - l[i][j] * l[k][j]

        def eliminate(c):
            for j in range(8):
                a = c[j]
                for k in range(j):
                    a = a - l[j][k] * c[k]
                c[j] = a * rinv[j]
            return c

        if g < 15:
            c1 = eliminate(ahead[0])
            diag = ahead[1]
            for j in range(8):
                for k in range(8):
                    diag[k] = diag[k] - c1[j] * wide(c1[j][k : k + 1, :])
        z = [None] * 8
        for j in range(8):
            row = wide(x_ref[r0 + j : r0 + j + 1, :])
            a = jnp.where(inside, jnp.where(lane == r0 + j, 1.0, 0.0), row)
            for k in range(j):
                a = a - l[j][k] * z[k]
            z[j] = a * rinv[j]
            d = jnp.where(lane < r0, 0.0, z[j])
            for k in range(j, 8):
                d = jnp.where(lane == r0 + k, l[k][j], d)
            if j:
                d = jnp.where(lane < r0 + j, 0.0, d)
            u_ref[r0 + j : r0 + j + 1, :] = d[:1]
            w_ref[r0 + j : r0 + j + 1, :] = jnp.where(lane < r0 + 8, z[j], 0.0)[:1]
        y = [None] * 8
        for j in reversed(range(8)):
            a = z[j]
            for i in range(j + 1, 8):
                a = a - l[i][j] * y[i]
            y[j] = a * rinv[j]
        for r in range(g + 1, 16):
            q = 8 * r
            x = x_ref[q : q + 8, :]
            if r == g + 1:
                c, v = c1, z
            else:
                c, v = cols(x, r0), y
            x = jnp.where(inside, 0.0, x)
            for j in range(8):
                x = x - c[j] * v[j]
            x_ref[q : q + 8, :] = x
            if r == g + 2:
                ahead = (cols(x, r0 + 8), cols(x, r0 + 16))


BY_ROW = [(r, c) for r in range(NP) for c in range(r + 1)]
BY_COL = [(r, c) for c in range(NP) for r in range(c, NP)]


def factor_kernel(spots, counts, k0, k1, live_at, take, s_ref, *refs):
    n_in = 2 * len(counts)
    ins = refs[:n_in]
    prev = refs[n_in : n_in + 5] if k0 else ()
    low_ref, lh_ref, ll_ref, wh_ref, wl_ref, a_s, l_s, d_s, w_s, u_s = refs[n_in + len(prev) :]
    live = s_ref[live_at]
    last = jnp.minimum(live, k1)
    first = 0
    for n, count in enumerate(counts):
        for t in range(count):
            r, c = spots[first + t]
            a_s[r * T : r * T + T, c * T : c * T + T] = ins[2 * n][t] + ins[2 * n + 1][t]
        first += count
    l_s[...] = jnp.zeros_like(l_s)
    ii = lax.broadcasted_iota(jnp.int32, (T, T), 0)
    jj = lax.broadcasted_iota(jnp.int32, (T, T), 1)
    eye = jnp.where(ii == jj, 1.0, 0.0).astype(f32)

    def dead(k, _):
        l_s[tl(k), tl(k)] = eye
        return 0

    lax.fori_loop(last, k1, dead, 0)
    tile_row = lax.broadcasted_iota(jnp.int32, (NP * T, T), 0) // T
    if k0:
        old = slice(0, k0 * T)
        for ref, src in zip((l_s, lh_ref, ll_ref), prev[:3]):
            ref[:, old] = src[...]
        for ref, src in zip((wh_ref, wl_ref), prev[3:]):
            ref[old, :] = src[...]

        def catch_up(j, _):
            xj = (prev[1][tl(j), :], prev[2][tl(j), :])
            a_s[:, tl(j)] = a_s[:, tl(j)] - dot3((prev[1][...], prev[2][...]), xj, NT)
            return 0

        lax.fori_loop(k0, last, catch_up, 0)

    def step(k, _):
        s = tl(k)
        d_s[...] = a_s[s, s]
        factor_tile(d_s, w_s, u_s)
        w = split(w_s[...])
        wh_ref[s, :] = w[0]
        wl_ref[s, :] = w[1]
        x = dot3(split(a_s[:, s]), w, NT)
        lh_ref[:, s], ll_ref[:, s] = split(x)
        l_s[:, s] = jnp.where((tile_row > k) & (tile_row < live), x, 0.0)
        l_s[s, s] = u_s[...].T

        def col(j, _):
            xj = (lh_ref[tl(j), s], ll_ref[tl(j), s])
            a_s[:, tl(j)] = a_s[:, tl(j)] - dot3((lh_ref[:, s], ll_ref[:, s]), xj, NT)
            return 0

        return lax.fori_loop(k + 1, last, col, 0)

    lax.fori_loop(k0, last, step, 0)
    if take is None:
        low_ref[...] = l_s[...]
    else:
        low_ref[...] = l_s[pl.ds(pl.multiple_of(take(s_ref), 64), low_ref.shape[0]), :]


def factor(scalars, pairs, spots, k0, k1, prev, live_at, take, rows):
    counts = tuple(x.shape[0] for x, _ in pairs)
    n = NP * T
    wide = k1 * T
    return call(
        functools.partial(factor_kernel, spots, counts, k0, k1, live_at, take),
        [scalars] + [x for pair in pairs for x in pair] + list(prev),
        [None] * (2 * len(pairs) + len(prev)),
        [shape(rows, wide), shape(n, wide, dtype=bf16), shape(n, wide, dtype=bf16)]
        + [shape(wide, T, dtype=bf16)] * 2,
        [pltpu.VMEM((n, wide), f32)] * 2 + [pltpu.VMEM((T, T), f32)] * 3,
        flops=20_000_000_000,
    )


def solve(x_ref, live, lh_ref, ll_ref, wh_ref, wl_ref, ph, plo, gh, gl):
    for m in range(NP // 2):
        a = slice(2 * m * T, 2 * m * T + T)
        b = slice(2 * m * T + T, 2 * m * T + 2 * T)
        for g, w in ((gh, wh_ref), (gl, wl_ref)):
            g[a, :T] = w[a, :]
            g[a, T:] = jnp.zeros((T, T), bf16)

        @pl.when(2 * m + 1 < live)
        def _():
            t = dot3((lh_ref[b, a], ll_ref[b, a]), (wh_ref[a, :], wl_ref[a, :]), NN)
            gh[b, :T], gl[b, :T] = split(-dot3((wh_ref[b, :], wl_ref[b, :]), split(t), NN))
            gh[b, T:] = wh_ref[b, :]
            gl[b, T:] = wl_ref[b, :]

        @pl.when(2 * m + 1 >= live)
        def _():
            gh[b, :] = jnp.zeros((T, 2 * T), bf16)
            gl[b, :] = jnp.zeros((T, 2 * T), bf16)

    for m in range(NP // 2):
        s = slice(2 * m * T, 2 * m * T + 2 * T)

        @pl.when(2 * m < live)
        def _():
            x = x_ref[:, s]
            if m:
                b = slice(0, 2 * m * T)
                x = x - dot3((ph[:, b], plo[:, b]), (lh_ref[s, b], ll_ref[s, b]), NT)
            x = dot3(split(x), (gh[s, :], gl[s, :]), NT)
            x_ref[:, s] = x
            ph[:, s], plo[:, s] = split(x)

        @pl.when(2 * m >= live)
        def _():
            x_ref[:, s] = jnp.zeros_like(x_ref[:, s])
            ph[:, s] = jnp.zeros_like(ph[:, s])
            plo[:, s] = jnp.zeros_like(plo[:, s])


def couple_one_kernel(s_ref, r_ref, c_ref, x_ref, inv):
    side = s_ref[SLO]
    invert(s_ref, OWN, NC, inv, 18)

    def tile(t, _):
        r = t // NP
        c = t % NP
        dst = (tl(r), tl(c))
        row = NP + side * 6 + r
        x_ref[dst] = r_ref[dst] * s_ref[FILL1 + t].astype(f32)

        @pl.when((inv[row] >= 0) & (inv[c] >= 0))
        def _():
            x_ref[dst] += c_ref[tl(inv[row]), tl(inv[c])]

        return 0

    lax.fori_loop(0, 36, tile, 0)


def panel_one_kernel(
    s_ref, x_ref, got_ref, lh, ll, wh, wl, p_ref, send_ref, ph, plo, gh, gl, inv2
):
    side = s_ref[SLO]
    invert(s_ref, OTH, NC, inv2, 18)
    p_ref[...] = x_ref[...]

    def tile(t, count):
        r = t // NP
        c = t % NP
        row = NP + side * 6 + r
        hit = (inv2[row] >= 0) & (inv2[c] >= 0)

        @pl.when(hit)
        def _():
            p_ref[tl(r), tl(c)] += got_ref[count]

        return count + hit.astype(jnp.int32)

    lax.fori_loop(0, 36, tile, 0)
    solve(p_ref, s_ref[LIVE1], lh, ll, wh, wl, ph, plo, gh, gl)
    send_ref[...] = p_ref[:, pl.ds(pl.multiple_of((1 - side) * 384, T), 384)]


def own_kernel(
    s_ref, p_ref, t0_ref, t1_ref, c_ref, pv_ref, own_ref, piv_ref, ph, plo, wide, inv, inv2
):
    side = s_ref[SLO]
    quarter = 2 * s_ref[SHI] + side
    ph[...], plo[...] = split(p_ref[...])
    for n in range(3):
        s = slice(n * 256, n * 256 + 256)
        base = jnp.where(side == 0, t0_ref[:, s], t1_ref[:, s])
        own_ref[:, s] = base - dot3((ph[...], plo[...]), (ph[s, :], plo[s, :]), NT)
    invert(s_ref, OWN, NC, inv, 18)
    invert(s_ref, MAP2, NU, inv2, 18)
    wide[...] = jnp.zeros_like(wide)
    wide[pl.ds(pl.multiple_of((quarter % 2) * 64, 64), 192), :] = pv_ref[...]
    base = (3 * quarter) // 2

    def emit(row, _):
        def col(c, _):
            at = row * (row + 1) // 2 + c
            source_tile(side, inv, inv2, own_ref, None, c_ref, piv_ref, at, row, c)

            @pl.when((row >= base) & (row < base + 2))
            def _():
                piv_ref[at] += wide[tl(row - base), tl(c)]

            return 0

        return lax.fori_loop(0, row + 1, col, 0)

    lax.fori_loop(0, NP, emit, 0)


def source_tile(side, inv, inv2, own_ref, cross_ref, c_ref, out_ref, at, r, c):
    i = inv2[r]
    j = inv2[c]
    used = (i >= 0) & (j >= 0)
    i = jnp.maximum(i, 0)
    j = jnp.maximum(j, 0)
    mi = (i // 6) == side
    mj = (j // 6) == side
    li = i % 6
    lj = j % 6

    @pl.when(used & mi & mj)
    def _():
        out_ref[at] = own_ref[tl(li), tl(lj)]

    if cross_ref is None:
        empty = jnp.logical_not(used & mi & mj)
    else:
        empty = jnp.logical_not(used) | (jnp.logical_not(mi) & jnp.logical_not(mj))

        @pl.when(used & mi & jnp.logical_not(mj))
        def _():
            out_ref[at] = cross_ref[tl(li), tl(lj)]

        @pl.when(used & jnp.logical_not(mi) & mj)
        def _():
            out_ref[at] = cross_ref[tl(lj), tl(li)].T

    @pl.when(empty)
    def _():
        out_ref[at] = jnp.zeros((T, T), f32)

    ci = inv[i + NP]
    cj = inv[j + NP]

    @pl.when(used & (ci >= 0) & (cj >= 0))
    def _():
        out_ref[at] += c_ref[tl(ci), tl(cj)]


def cross_kernel(s_ref, p_ref, q_ref, t1_ref, piv_ref, cross_ref, a_ref, b_ref, inv2):
    side = s_ref[SLO]
    pc = split(p_ref[...])
    qh, ql = split(q_ref[...])
    for n in range(3):
        s = slice(n * 256, n * 256 + 256)
        base = jnp.where(side == 0, t1_ref[:, s], 0.0)
        cross_ref[:, s] = base - dot3(pc, (qh[s, :], ql[s, :]), NT)
    invert(s_ref, MAP2, NU, inv2, 18)
    a_ref[...] = piv_ref[0:10]
    b_ref[...] = piv_ref[10:21]

    def emit(out_ref, first, row):
        def col(c, _):
            at = row * (row + 1) // 2 + c - first
            i = inv2[row]
            j = inv2[c]
            used = (i >= 0) & (j >= 0)
            i = jnp.maximum(i, 0)
            j = jnp.maximum(j, 0)
            mi = (i // 6) == side
            mj = (j // 6) == side

            @pl.when(used & mi & jnp.logical_not(mj))
            def _():
                out_ref[at] += cross_ref[tl(i % 6), tl(j % 6)]

            @pl.when(used & jnp.logical_not(mi) & mj)
            def _():
                out_ref[at] += cross_ref[tl(j % 6), tl(i % 6)].T

            return 0

        lax.fori_loop(0, row + 1, col, 0)

    lax.fori_loop(0, 4, lambda r, _: (emit(a_ref, 0, r), 0)[1], 0)
    lax.fori_loop(4, 6, lambda r, _: (emit(b_ref, 10, r), 0)[1], 0)


def rows_two_kernel(first, width, s_ref, own_ref, cross_ref, c_ref, *refs):
    outs = refs[:4]
    inv, inv2 = refs[4:]
    lo = s_ref[SLO]
    hi = s_ref[SHI]
    invert(s_ref, OWN, NC, inv, 18)
    invert(s_ref, MAP2, NU, inv2, 18)
    half = width // 2
    orders = (
        (0, (1 - hi, 1 - lo), (1 - hi, lo)),
        (0, (hi, 1 - lo), (hi, lo)),
        (half, (1 - hi, 1 - lo), (hi, 1 - lo)),
        (half, (1 - hi, lo), (hi, lo)),
    )
    for out_ref, (skip, one, two) in zip(outs, orders):

        def tile(t, _):
            r = t // half
            later = (r >= 3).astype(jnp.int32)
            a = one[0] + (two[0] - one[0]) * later
            b = one[1] + (two[1] - one[1]) * later
            row = NP + 6 * a + 3 * b + r % 3
            col = first + skip + t % half
            source_tile(lo, inv, inv2, own_ref, cross_ref, c_ref, out_ref, t, row, col)
            return 0

        lax.fori_loop(0, 6 * half, tile, 0)


def rows_two(scalars, own, cross, block_c, first, width):
    count = 3 * width
    return call(
        functools.partial(rows_two_kernel, first, width),
        [scalars, own, cross, block_c],
        [None] * 3,
        [shape(count, T, T)] * 4,
        [pltpu.SMEM((18,), jnp.int32)] * 2,
    )


NINE = [(r, c) for r in range(3) for c in range(3)]
DX, DZ = [(0, 0), (1, 0), (1, 1)], [(2, 0), (2, 1), (2, 2)]
GX, GZ = NINE[:4], NINE[4:]


def chain_x(m, x, z, d):
    return (
        [(z, z, t) for t in DX]
        + [(z, x, t) for t in GX]
        + [(m, z, t) for t in NINE]
        + [(m, m, t) for t in DX]
        + [(m, d, t) for t in GX]
    )


def chain_z(m, x, z, d):
    return (
        [(x, x, t) for t in DZ]
        + [(x, z, t) for t in GZ]
        + [(m, x, t) for t in NINE]
        + [(m, m, t) for t in DZ]
        + [(m, d, t) for t in GZ]
    )


def trailing_two_kernel(
    s_ref, own_ref, cross_ref, c_ref, xs, xk, zs, zk, inv, inv2, rtab, ctab
):
    lo = s_ref[SLO]
    hi = s_ref[SHI]
    invert(s_ref, OWN, NC, inv, 18)
    invert(s_ref, MAP2, NU, inv2, 18)
    m, x, z, d = (
        NP + 3 * (2 * a + b) for a, b in ((hi, lo), (1 - hi, lo), (hi, 1 - lo), (1 - hi, 1 - lo))
    )
    for out_ref, tiles in (
        (xs, chain_x(x, m, d, z)),
        (xk, chain_x(m, x, z, d)),
        (zs, chain_z(z, d, m, x)),
        (zk, chain_z(m, x, z, d)),
    ):
        for n, (rq, cq, (r, c)) in enumerate(tiles):
            rtab[n] = rq + r
            ctab[n] = cq + c

        def tile(t, _):
            source_tile(lo, inv, inv2, own_ref, cross_ref, c_ref, out_ref, t, rtab[t], ctab[t])
            return 0

        lax.fori_loop(0, len(tiles), tile, 0)


def panel_two_kernel(
    s_ref, r_ref, xk, x1, x2, zk, z1, z2, lh, ll, wh, wl, p_ref, ph, plo, gh, gl
):
    for r in range(3):
        for c in range(3):
            t = 3 * r + c
            dst = (slice(r * T, r * T + T), slice(c * T, c * T + T))
            fill = s_ref[FILL2 + 6 * r + c].astype(f32)
            p_ref[dst] = r_ref[dst] * fill + ((xk[9 + t] + x1[9 + t]) + x2[t])
            dst = (dst[0], slice((c + 3) * T, (c + 4) * T))
            fill = s_ref[FILL2 + 6 * r + c + 3].astype(f32)
            p_ref[dst] = r_ref[dst] * fill + ((zk[9 + t] + z1[9 + t]) + z2[t])
    solve(p_ref, s_ref[LIVE2], lh, ll, wh, wl, ph, plo, gh, gl)


def schur_base_kernel(s_ref, r_ref, p_ref, xk, x1, x2, zk, z1, z2, out_ref):
    hi = s_ref[SHI]
    lo = s_ref[SLO]
    out_ref[...] = r_ref[:, NP * T :]
    m, x, z, d = (
        3 * (2 * a + b) for a, b in ((hi, lo), (1 - hi, lo), (hi, 1 - lo), (1 - hi, 1 - lo))
    )
    mine = split(p_ref[...])
    cols = pl.ds(pl.multiple_of(m * T, T), 384)
    out_ref[:, cols] = out_ref[:, cols] - dot3(mine, mine, NT)

    def add(quarter, r, c, value):
        out_ref[r * T : r * T + T, tl(quarter + c)] += value

    for k, r1, r2, diag, cross, pair in ((xk, x1, x2, DX, GX, z), (zk, z1, z2, DZ, GZ, x)):
        nd = len(diag)
        ng = len(cross)
        base = nd + ng + 9
        for n, (r, c) in enumerate(diag):
            v = (k[base + n] + r1[base + n]) + r2[n]
            add(m, r, c, v)
            if r != c:
                add(m, c, r, v.T)
        for n, (r, c) in enumerate(cross):
            v = (k[base + nd + n] + r1[base + nd + n]) + r2[nd + n]
            add(d, r, c, v)
        for n, (r, c) in enumerate(NINE):
            v = (k[nd + ng + n] + r1[nd + ng + n]) + r2[nd + ng + 3 * c + r].T
            add(pair, r, c, v)


def schur_near_kernel(s_ref, b_ref, p_ref, px, pz, out_ref):
    hi = s_ref[SHI]
    lo = s_ref[SLO]
    mine = split(p_ref[...])
    out_ref[...] = b_ref[...]
    for a, b, other in ((1 - hi, lo, px), (hi, 1 - lo, pz)):
        cols = pl.ds(pl.multiple_of((2 * a + b) * 384, T), 384)
        out_ref[:, cols] = b_ref[:, cols] - dot3(mine, split(other[...]), NT)


def schur_far_kernel(s_ref, b_ref, p_ref, pd0, pd1, out_ref):
    other = split(jnp.concatenate([pd0[...], pd1[...]], axis=0))
    out_ref[...] = b_ref[...] - dot3(split(p_ref[...]), other, NT)


def across(axis, values):
    size = lax.axis_size(axis)
    return lax.ppermute(values, axis, [(i, i ^ (size // 2)) for i in range(size)])


def program(
    contribution,
    pivot_one,
    rows_one,
    pivot_two,
    rows_two_in,
    map_one,
    map_two,
    fill_one,
    fill_two,
    live_one,
    live_two,
):
    size_lo = lax.axis_size("lo")
    size_hi = lax.axis_size("hi")
    half_lo = size_lo // 2
    half_hi = size_hi // 2
    lo = lax.axis_index("lo")
    hi = lax.axis_index("hi")
    side_lo = lo // half_lo
    side_hi = hi // half_hi
    front_lo = lo % half_lo
    front_hi = hi % half_hi
    quarter = 2 * side_hi + side_lo
    i32 = jnp.int32
    c = contribution[0, 0]
    rows1 = rows_one[0, 0]
    rows2 = rows_two_in[0, 0]
    smem = pltpu.SMEM((18,), i32)
    n = NP * T

    own_map = map_one[hi, lo]
    (piv_a,) = call(
        functools.partial(gather_a_kernel, half_lo),
        [own_map, c, pivot_one[0, 0]],
        [None, block(384, 256, 0)],
        [shape(11, T, T)],
        [smem],
    )
    piv_a, map_one, map_two, fill_one, fill_two, live_one, live_two, own_map = (
        lax.optimization_barrier(
            (piv_a, map_one, map_two, fill_one, fill_two, live_one, live_two, own_map)
        )
    )
    got_a = across("lo", piv_a)
    piv_b, coup = call(
        functools.partial(gather_b_kernel, half_lo),
        [own_map, c, pivot_one[0, 0]],
        [None, None],
        [shape(10, T, T), shape(16, T, T)],
        [smem],
    )
    scalars = jnp.concatenate(
        [
            map_one[hi, lo],
            map_one[hi, (lo + half_lo) % size_lo],
            map_two[hi, front_lo],
            jnp.stack([side_lo, side_hi]).astype(i32),
            live_one[hi, front_lo][None],
            live_two[front_hi, front_lo][None],
            lax.dynamic_slice_in_dim(fill_one[hi, front_lo], side_lo * 6, 6, 0).reshape(36),
            lax.dynamic_slice_in_dim(fill_two[front_hi, front_lo], quarter * 3, 3, 0).reshape(18),
        ]
    )
    piv_b, got_a = lax.optimization_barrier((piv_b, got_a))
    got_b = across("lo", piv_b)
    part = factor(scalars, [(piv_a, got_a)], BY_COL, 0, 2, (), LIVE1, None, n)
    later, *part = lax.optimization_barrier((scalars, *part))
    (x_one,) = call(
        couple_one_kernel,
        [later, rows1, c],
        [block(n, n, 0), None],
        [shape(n, n)],
        [smem],
    )
    coup, got_b = lax.optimization_barrier((coup, got_b))
    coup_got = across("lo", coup)
    lower_one, *fac1 = factor(
        scalars,
        [(piv_b, got_b)],
        BY_COL[11:],
        2,
        NP,
        part,
        LIVE1,
        lambda s: s[SLO] * 384,
        384,
    )
    panel_one, send = call(
        panel_one_kernel,
        [scalars, x_one, coup_got, *fac1],
        [None] * 6,
        [shape(n, n), shape(n, n // 2)],
        [pltpu.VMEM((n, n), bf16)] * 2 + [pltpu.VMEM((n, 2 * T), bf16)] * 2 + [smem],
        flops=3_000_000_000,
    )
    got = across("lo", send)
    own, piv = call(
        own_kernel,
        [scalars, panel_one, rows1, rows1, c, pivot_two[0, 0]],
        [None, block(n, n, 1), block(n, n, 2), None, None],
        [shape(n, n), shape(21, T, T)],
        [pltpu.VMEM((n, n), bf16)] * 2 + [pltpu.VMEM((2 * T, n), f32), smem, smem],
        flops=4_000_000_000,
    )
    cross, pa, pb = call(
        cross_kernel,
        [scalars, panel_one, got, rows1, piv],
        [pl.BlockSpec((n, n // 2), lambda i, s: (0, s[SLO])), None, block(n, n, 2), None],
        [shape(n, n), shape(10, T, T), shape(11, T, T)],
        [smem],
        flops=2_000_000_000,
    )
    pa1 = across("hi", pa)
    pb1 = across("lo", pb)
    pa, pb, cross = lax.optimization_barrier((pa, pb, cross))
    cxs, cxk, czs, czk = rows_two(scalars, own, cross, c, 0, NP)
    pa = pa + pa1
    pb = pb + pb1
    pa, pb, cxs, czs = lax.optimization_barrier((pa, pb, cxs, czs))
    pa2 = across("lo", pa)
    pb2 = across("hi", pb)
    cx1 = across("hi", cxs)
    cz1 = across("lo", czs)
    txs, txk, tzs, tzk = call(
        trailing_two_kernel,
        [scalars, own, cross, c],
        [None] * 3,
        [shape(23, T, T)] * 2 + [shape(25, T, T)] * 2,
        [smem, smem] + [pltpu.SMEM((32,), i32)] * 2,
    )
    tx1 = across("hi", txs)
    tz1 = across("lo", tzs)
    lower_two, *fac2 = factor(
        scalars,
        [(pa, pa2), (pb, pb2)],
        BY_ROW,
        0,
        NP,
        (),
        LIVE2,
        lambda s: (2 * s[SHI] + s[SLO]) * 192,
        192,
    )
    cx2 = across("lo", cxk[:9] + cx1[:9])
    cz2 = across("hi", czk[:9] + cz1[:9])
    tx = txk[:16] + tx1[:16]
    tz = tzk[:17] + tz1[:17]
    tx2 = across("lo", tx)
    tz2 = across("hi", tz)
    (panel_two,) = call(
        panel_two_kernel,
        [scalars, rows2, cxk, cx1, cx2, czk, cz1, cz2, *fac2],
        [block(384, n, 0)] + [None] * 10,
        [shape(384, n)],
        [pltpu.VMEM((384, n), bf16)] * 2 + [pltpu.VMEM((n, 2 * T), bf16)] * 2,
        flops=2_000_000_000,
    )
    px = across("hi", panel_two)
    pz = across("lo", panel_two)
    pd0 = across("hi", pz[:192])
    pd1 = across("lo", px[192:])
    (base_two,) = call(
        schur_base_kernel,
        [scalars, rows2, panel_two, txk, tx1, tx2, tzk, tz1, tz2],
        [None] * 8,
        [shape(384, NU * T)],
        [],
        flops=1_000_000_000,
    )
    (near_two,) = call(
        schur_near_kernel,
        [scalars, base_two, panel_two, px, pz],
        [None] * 4,
        [shape(384, NU * T)],
        [],
        flops=2_000_000_000,
    )
    far = pl.BlockSpec((384, 384), lambda i, s: (0, 2 * (1 - s[SHI]) + 1 - s[SLO]))
    (schur_two,) = call(
        schur_far_kernel,
        [scalars, near_two, panel_two, pd0, pd1],
        [far, None, None, None],
        [shape(384, NU * T)],
        [],
        flops=1_000_000_000,
        out_specs=[far],
        aliases={1: 0},
    )
    return tuple(
        out[None, None] for out in (lower_one, panel_one, lower_two, panel_two, schur_two)
    )


def solution(mesh):
    split_spec = P("hi", "lo", None, None)
    return jax.shard_map(
        program,
        mesh=mesh,
        in_specs=(split_spec,) * 5 + (P(),) * 6,
        out_specs=(split_spec,) * 5,
        check_vma=False,
    )
```

```python
import functools
import jax
import jax.numpy as jnp
from jax import lax
from jax.experimental import pallas as pl
from jax.experimental.pallas import tpu as pltpu
from jax.sharding import PartitionSpec as P


T = 128
NP = 6
NU = 12
NC = 8
f32 = jnp.float32
bf16 = jnp.bfloat16
NN = ((1,), (0,))
NT = ((1,), (1,))
OWN, OTH, MAP2, SLO, SHI, LIVE1, LIVE2, FILL1, FILL2 = 0, 8, 16, 28, 29, 30, 31, 32, 68


def tl(i):
    if isinstance(i, int):
        return slice(i * T, i * T + T)
    return pl.ds(pl.multiple_of(i * T, T), T)


def split(x):
    hi = x.astype(bf16)
    return hi, (x - hi.astype(f32)).astype(bf16)


def dot3(a, b, dims):
    (ah, al), (bh, bl) = a, b
    dn = (dims, ((), ()))
    f = lambda x, y: lax.dot_general(x, y, dn, preferred_element_type=f32)
    return f(ah, bh) + (f(ah, bl) + f(al, bh))


def call(kernel, args, specs, outs, scratch, flops=0, out_specs=None, aliases=None):
    whole = pl.BlockSpec(memory_space=pltpu.VMEM)
    in_specs = [whole if s is None else s for s in specs]
    nbytes = sum(4 * a.size for a in args[1:]) + sum(4 * o.size for o in outs)
    return pl.pallas_call(
        kernel,
        grid_spec=pltpu.PrefetchScalarGridSpec(
            num_scalar_prefetch=1,
            grid=(1,),
            in_specs=in_specs,
            out_specs=out_specs or [whole] * len(outs),
            scratch_shapes=scratch,
        ),
        out_shape=outs,
        input_output_aliases=aliases or {},
        compiler_params=pltpu.CompilerParams(vmem_limit_bytes=60 * 1024 * 1024),
        cost_estimate=pl.CostEstimate(flops=flops, bytes_accessed=nbytes, transcendentals=0),
    )(*args)


def shape(*dims, dtype=f32):
    return jax.ShapeDtypeStruct(dims, dtype)


def block(rows, cols, j):
    return pl.BlockSpec((rows, cols), lambda i, s: (0, j))


def invert(s_ref, first, count, inv_ref, size):
    for r in range(size):
        inv_ref[r] = -1
    for i in range(count):
        inv_ref[s_ref[first + i]] = i


def gather_tiles(side, inv, c_ref, p_ref, out_ref, first, last, skip):
    for c in range(first, last):
        base = BY_COL.index((c, c)) - skip - c

        def tile(r, _):
            at = base + r
            local = r - 3 * side

            @pl.when((local >= 0) & (local < 3))
            def _():
                out_ref[at] = p_ref[tl(local), tl(c)]

            @pl.when((local < 0) | (local >= 3))
            def _():
                out_ref[at] = jnp.zeros((T, T), f32)

            @pl.when((inv[r] >= 0) & (inv[c] >= 0))
            def _():
                out_ref[at] += c_ref[tl(inv[r]), tl(inv[c])]

            return 0

        lax.fori_loop(c, NP, tile, 0)


def gather_a_kernel(half_lo, s_ref, c_ref, p_ref, a_ref, inv):
    side = lax.axis_index("lo") // half_lo
    invert(s_ref, OWN, NC, inv, 18)
    gather_tiles(side, inv, c_ref, p_ref, a_ref, 0, 2, 0)


def gather_b_kernel(half_lo, s_ref, c_ref, p_ref, b_ref, coup_ref, inv):
    side = lax.axis_index("lo") // half_lo
    invert(s_ref, OWN, NC, inv, 18)
    gather_tiles(side, inv, c_ref, p_ref, b_ref, 2, NP, 11)

    def coup_tile(t, count):
        row = inv[NP + (1 - side) * 6 + t // NP]
        col = inv[t % NP]
        hit = (row >= 0) & (col >= 0)

        @pl.when(hit)
        def _():
            coup_ref[count] = c_ref[tl(row), tl(col)]

        return count + hit.astype(jnp.int32)

    lax.fori_loop(0, 36, coup_tile, 0)


def factor_tile(x_ref, w_ref, u_ref):
    lane = lax.broadcasted_iota(jnp.int32, (8, T), 1)
    wide = lambda v: jnp.broadcast_to(v, (8, T))
    cols = lambda x, r0: [wide(x[:, r0 + k : r0 + k + 1]) for k in range(8)]
    diag = cols(x_ref[0:8, :], 0)
    x = x_ref[8:16, :]
    ahead = (cols(x, 0), cols(x, 8))
    for g in range(16):
        r0 = 8 * g
        inside = (lane >= r0) & (lane < r0 + 8)
        e = [[wide(diag[k][i : i + 1, :]) for k in range(i + 1)] for i in range(8)]
        l = [[None] * 8 for _ in range(8)]
        rinv = [None] * 8
        for j in range(8):
            rinv[j] = lax.rsqrt(e[j][j])
            l[j][j] = e[j][j] * rinv[j]
            for i in range(j + 1, 8):
                l[i][j] = e[i][j] * rinv[j]
            for i in range(j + 1, 8):
                for k in range(j + 1, i + 1):
                    e[i][k] = e[i][k] - l[i][j] * l[k][j]

        def eliminate(c):
            for j in range(8):
                a = c[j]
                for k in range(j):
                    a = a - l[j][k] * c[k]
                c[j] = a * rinv[j]
            return c

        if g < 15:
            c1 = eliminate(ahead[0])
            diag = ahead[1]
            for j in range(8):
                for k in range(8):
                    diag[k] = diag[k] - c1[j] * wide(c1[j][k : k + 1, :])
        z = [None] * 8
        for j in range(8):
            row = wide(x_ref[r0 + j : r0 + j + 1, :])
            a = jnp.where(inside, jnp.where(lane == r0 + j, 1.0, 0.0), row)
            for k in range(j):
                a = a - l[j][k] * z[k]
            z[j] = a * rinv[j]
            d = jnp.where(lane < r0, 0.0, z[j])
            for k in range(j, 8):
                d = jnp.where(lane == r0 + k, l[k][j], d)
            if j:
                d = jnp.where(lane < r0 + j, 0.0, d)
            u_ref[r0 + j : r0 + j + 1, :] = d[:1]
            w_ref[r0 + j : r0 + j + 1, :] = jnp.where(lane < r0 + 8, z[j], 0.0)[:1]
        y = [None] * 8
        for j in reversed(range(8)):
            a = z[j]
            for i in range(j + 1, 8):
                a = a - l[i][j] * y[i]
            y[j] = a * rinv[j]
        for r in range(g + 1, 16):
            q = 8 * r
            x = x_ref[q : q + 8, :]
            if r == g + 1:
                c, v = c1, z
            else:
                c, v = cols(x, r0), y
            x = jnp.where(inside, 0.0, x)
            for j in range(8):
                x = x - c[j] * v[j]
            x_ref[q : q + 8, :] = x
            if r == g + 2:
                ahead = (cols(x, r0 + 8), cols(x, r0 + 16))


BY_ROW = [(r, c) for r in range(NP) for c in range(r + 1)]
BY_COL = [(r, c) for c in range(NP) for r in range(c, NP)]


def factor_kernel(spots, counts, k0, k1, live_at, take, s_ref, *refs):
    n_in = 2 * len(counts)
    ins = refs[:n_in]
    prev = refs[n_in : n_in + 5] if k0 else ()
    low_ref, lh_ref, ll_ref, wh_ref, wl_ref, a_s, l_s, d_s, w_s, u_s = refs[n_in + len(prev) :]
    live = s_ref[live_at]
    last = jnp.minimum(live, k1)
    first = 0
    for n, count in enumerate(counts):
        for t in range(count):
            r, c = spots[first + t]
            a_s[r * T : r * T + T, c * T : c * T + T] = ins[2 * n][t] + ins[2 * n + 1][t]
        first += count
    l_s[...] = jnp.zeros_like(l_s)
    ii = lax.broadcasted_iota(jnp.int32, (T, T), 0)
    jj = lax.broadcasted_iota(jnp.int32, (T, T), 1)
    eye = jnp.where(ii == jj, 1.0, 0.0).astype(f32)

    def dead(k, _):
        l_s[tl(k), tl(k)] = eye
        return 0

    lax.fori_loop(last, k1, dead, 0)
    tile_row = lax.broadcasted_iota(jnp.int32, (NP * T, T), 0) // T
    if k0:
        old = slice(0, k0 * T)
        for ref, src in zip((l_s, lh_ref, ll_ref), prev[:3]):
            ref[:, old] = src[...]
        for ref, src in zip((wh_ref, wl_ref), prev[3:]):
            ref[old, :] = src[...]

        def catch_up(j, _):
            xj = (prev[1][tl(j), :], prev[2][tl(j), :])
            a_s[:, tl(j)] = a_s[:, tl(j)] - dot3((prev[1][...], prev[2][...]), xj, NT)
            return 0

        lax.fori_loop(k0, last, catch_up, 0)

    def step(k, _):
        s = tl(k)
        d_s[...] = a_s[s, s]
        factor_tile(d_s, w_s, u_s)
        w = split(w_s[...])
        wh_ref[s, :] = w[0]
        wl_ref[s, :] = w[1]
        x = dot3(split(a_s[:, s]), w, NT)
        lh_ref[:, s], ll_ref[:, s] = split(x)
        l_s[:, s] = jnp.where((tile_row > k) & (tile_row < live), x, 0.0)
        l_s[s, s] = u_s[...].T

        def col(j, _):
            xj = (lh_ref[tl(j), s], ll_ref[tl(j), s])
            a_s[:, tl(j)] = a_s[:, tl(j)] - dot3((lh_ref[:, s], ll_ref[:, s]), xj, NT)
            return 0

        return lax.fori_loop(k + 1, last, col, 0)

    lax.fori_loop(k0, last, step, 0)
    if take is None:
        low_ref[...] = l_s[...]
    else:
        low_ref[...] = l_s[pl.ds(pl.multiple_of(take(s_ref), 64), low_ref.shape[0]), :]


def factor(scalars, pairs, spots, k0, k1, prev, live_at, take, rows):
    counts = tuple(x.shape[0] for x, _ in pairs)
    n = NP * T
    wide = k1 * T
    return call(
        functools.partial(factor_kernel, spots, counts, k0, k1, live_at, take),
        [scalars] + [x for pair in pairs for x in pair] + list(prev),
        [None] * (2 * len(pairs) + len(prev)),
        [shape(rows, wide), shape(n, wide, dtype=bf16), shape(n, wide, dtype=bf16)]
        + [shape(wide, T, dtype=bf16)] * 2,
        [pltpu.VMEM((n, wide), f32)] * 2 + [pltpu.VMEM((T, T), f32)] * 3,
        flops=20_000_000_000,
    )


def solve(x_ref, live, lh_ref, ll_ref, wh_ref, wl_ref, ph, plo, gh, gl):
    for m in range(NP // 2):
        a = slice(2 * m * T, 2 * m * T + T)
        b = slice(2 * m * T + T, 2 * m * T + 2 * T)
        for g, w in ((gh, wh_ref), (gl, wl_ref)):
            g[a, :T] = w[a, :]
            g[a, T:] = jnp.zeros((T, T), bf16)

        @pl.when(2 * m + 1 < live)
        def _():
            t = dot3((lh_ref[b, a], ll_ref[b, a]), (wh_ref[a, :], wl_ref[a, :]), NN)
            gh[b, :T], gl[b, :T] = split(-dot3((wh_ref[b, :], wl_ref[b, :]), split(t), NN))
            gh[b, T:] = wh_ref[b, :]
            gl[b, T:] = wl_ref[b, :]

        @pl.when(2 * m + 1 >= live)
        def _():
            gh[b, :] = jnp.zeros((T, 2 * T), bf16)
            gl[b, :] = jnp.zeros((T, 2 * T), bf16)

    for m in range(NP // 2):
        s = slice(2 * m * T, 2 * m * T + 2 * T)

        @pl.when(2 * m < live)
        def _():
            x = x_ref[:, s]
            if m:
                b = slice(0, 2 * m * T)
                x = x - dot3((ph[:, b], plo[:, b]), (lh_ref[s, b], ll_ref[s, b]), NT)
            x = dot3(split(x), (gh[s, :], gl[s, :]), NT)
            x_ref[:, s] = x
            ph[:, s], plo[:, s] = split(x)

        @pl.when(2 * m >= live)
        def _():
            x_ref[:, s] = jnp.zeros_like(x_ref[:, s])
            ph[:, s] = jnp.zeros_like(ph[:, s])
            plo[:, s] = jnp.zeros_like(plo[:, s])


def couple_one_kernel(s_ref, r_ref, c_ref, x_ref, inv):
    side = s_ref[SLO]
    invert(s_ref, OWN, NC, inv, 18)

    def tile(t, _):
        r = t // NP
        c = t % NP
        dst = (tl(r), tl(c))
        row = NP + side * 6 + r
        x_ref[dst] = r_ref[dst] * s_ref[FILL1 + t].astype(f32)

        @pl.when((inv[row] >= 0) & (inv[c] >= 0))
        def _():
            x_ref[dst] += c_ref[tl(inv[row]), tl(inv[c])]

        return 0

    lax.fori_loop(0, 36, tile, 0)


def panel_one_kernel(
    s_ref, x_ref, got_ref, lh, ll, wh, wl, p_ref, send_ref, ph, plo, gh, gl, inv2
):
    side = s_ref[SLO]
    invert(s_ref, OTH, NC, inv2, 18)
    p_ref[...] = x_ref[...]

    def tile(t, count):
        r = t // NP
        c = t % NP
        row = NP + side * 6 + r
        hit = (inv2[row] >= 0) & (inv2[c] >= 0)

        @pl.when(hit)
        def _():
            p_ref[tl(r), tl(c)] += got_ref[count]

        return count + hit.astype(jnp.int32)

    lax.fori_loop(0, 36, tile, 0)
    solve(p_ref, s_ref[LIVE1], lh, ll, wh, wl, ph, plo, gh, gl)
    send_ref[...] = p_ref[:, pl.ds(pl.multiple_of((1 - side) * 384, T), 384)]


def mixed(side, inv2, r, c):
    i = inv2[r]
    j = inv2[c]
    used = (i >= 0) & (j >= 0)
    i = jnp.maximum(i, 0)
    j = jnp.maximum(j, 0)
    mi = (i // 6) == side
    mj = (j // 6) == side
    return i % 6, j % 6, used & mi & jnp.logical_not(mj), used & jnp.logical_not(mi) & mj


def own_kernel(
    s_ref, p_ref, t0_ref, t1_ref, c_ref, pv_ref, own_ref, piv_ref, ph, plo, wide, inv, inv2
):
    side = s_ref[SLO]
    quarter = 2 * s_ref[SHI] + side
    ph[...], plo[...] = split(p_ref[...])
    for n in range(3):
        s = slice(n * 256, n * 256 + 256)
        base = jnp.where(side == 0, t0_ref[:, s], t1_ref[:, s])
        own_ref[:, s] = base - dot3((ph[...], plo[...]), (ph[s, :], plo[s, :]), NT)
    invert(s_ref, OWN, NC, inv, 18)
    invert(s_ref, MAP2, NU, inv2, 18)
    wide[...] = jnp.zeros_like(wide)
    wide[pl.ds(pl.multiple_of((quarter % 2) * 64, 64), 192), :] = pv_ref[...]
    base = (3 * quarter) // 2

    def emit(row, _):
        def col(c, _):
            at = row * (row + 1) // 2 + c
            source_tile(side, inv, inv2, own_ref, None, c_ref, piv_ref, at, row, c)
            i, j, ahead, behind = mixed(side, inv2, row, c)

            @pl.when(ahead & (side == 0))
            def _():
                piv_ref[at] += t1_ref[tl(i), tl(j)]

            @pl.when(behind & (side == 0))
            def _():
                piv_ref[at] += t1_ref[tl(j), tl(i)].T

            @pl.when((row >= base) & (row < base + 2))
            def _():
                piv_ref[at] += wide[tl(row - base), tl(c)]

            return 0

        return lax.fori_loop(0, row + 1, col, 0)

    lax.fori_loop(0, NP, emit, 0)


def source_tile(side, inv, inv2, own_ref, cross_ref, c_ref, out_ref, at, r, c):
    i = inv2[r]
    j = inv2[c]
    used = (i >= 0) & (j >= 0)
    i = jnp.maximum(i, 0)
    j = jnp.maximum(j, 0)
    mi = (i // 6) == side
    mj = (j // 6) == side
    li = i % 6
    lj = j % 6

    @pl.when(used & mi & mj)
    def _():
        out_ref[at] = own_ref[tl(li), tl(lj)]

    if cross_ref is None:
        empty = jnp.logical_not(used & mi & mj)
    else:
        empty = jnp.logical_not(used) | (jnp.logical_not(mi) & jnp.logical_not(mj))

        @pl.when(used & mi & jnp.logical_not(mj))
        def _():
            out_ref[at] = cross_ref[tl(li), tl(lj)]

        @pl.when(used & jnp.logical_not(mi) & mj)
        def _():
            out_ref[at] = cross_ref[tl(lj), tl(li)].T

    @pl.when(empty)
    def _():
        out_ref[at] = jnp.zeros((T, T), f32)

    ci = inv[i + NP]
    cj = inv[j + NP]

    @pl.when(used & (ci >= 0) & (cj >= 0))
    def _():
        out_ref[at] += c_ref[tl(ci), tl(cj)]


def cross_pivot_kernel(s_ref, p_ref, q_ref, piv_ref, a_ref, b_ref, inv2):
    side = s_ref[SLO]
    invert(s_ref, MAP2, NU, inv2, 18)
    a_ref[...] = piv_ref[0:10]
    b_ref[...] = piv_ref[10:21]

    def emit(out_ref, first, row):
        def col(c, _):
            at = row * (row + 1) // 2 + c - first
            i, j, ahead, behind = mixed(side, inv2, row, c)

            @pl.when(ahead)
            def _():
                out_ref[at] -= dot3(split(p_ref[tl(i), :]), split(q_ref[tl(j), :]), NT)

            @pl.when(behind)
            def _():
                out_ref[at] -= dot3(split(q_ref[tl(i), :]), split(p_ref[tl(j), :]), NT)

            return 0

        lax.fori_loop(0, row + 1, col, 0)

    lax.fori_loop(0, 4, lambda r, _: (emit(a_ref, 0, r), 0)[1], 0)
    lax.fori_loop(4, 6, lambda r, _: (emit(b_ref, 10, r), 0)[1], 0)


def cross_kernel(s_ref, p_ref, q_ref, t1_ref, cross_ref):
    side = s_ref[SLO]
    pc = split(p_ref[...])
    qh, ql = split(q_ref[...])
    for n in range(3):
        s = slice(n * 256, n * 256 + 256)
        base = jnp.where(side == 0, t1_ref[:, s], 0.0)
        cross_ref[:, s] = base - dot3(pc, (qh[s, :], ql[s, :]), NT)


def rows_two_kernel(first, width, s_ref, own_ref, cross_ref, c_ref, *refs):
    outs = refs[:4]
    inv, inv2 = refs[4:]
    lo = s_ref[SLO]
    hi = s_ref[SHI]
    invert(s_ref, OWN, NC, inv, 18)
    invert(s_ref, MAP2, NU, inv2, 18)
    half = width // 2
    orders = (
        (0, (1 - hi, 1 - lo), (1 - hi, lo)),
        (0, (hi, 1 - lo), (hi, lo)),
        (half, (1 - hi, 1 - lo), (hi, 1 - lo)),
        (half, (1 - hi, lo), (hi, lo)),
    )
    for out_ref, (skip, one, two) in zip(outs, orders):

        def tile(t, _):
            r = t // half
            later = (r >= 3).astype(jnp.int32)
            a = one[0] + (two[0] - one[0]) * later
            b = one[1] + (two[1] - one[1]) * later
            row = NP + 6 * a + 3 * b + r % 3
            col = first + skip + t % half
            source_tile(lo, inv, inv2, own_ref, cross_ref, c_ref, out_ref, t, row, col)
            return 0

        lax.fori_loop(0, 6 * half, tile, 0)


def rows_two(scalars, own, cross, block_c, first, width):
    count = 3 * width
    return call(
        functools.partial(rows_two_kernel, first, width),
        [scalars, own, cross, block_c],
        [None] * 3,
        [shape(count, T, T)] * 4,
        [pltpu.SMEM((18,), jnp.int32)] * 2,
    )


NINE = [(r, c) for r in range(3) for c in range(3)]
DX, DZ = [(0, 0), (1, 0), (1, 1)], [(2, 0), (2, 1), (2, 2)]
GX, GZ = NINE[:4], NINE[4:]


def chain_x(m, x, z, d):
    return (
        [(z, z, t) for t in DX]
        + [(z, x, t) for t in GX]
        + [(m, z, t) for t in NINE]
        + [(m, m, t) for t in DX]
        + [(m, d, t) for t in GX]
    )


def chain_z(m, x, z, d):
    return (
        [(x, x, t) for t in DZ]
        + [(x, z, t) for t in GZ]
        + [(m, x, t) for t in NINE]
        + [(m, m, t) for t in DZ]
        + [(m, d, t) for t in GZ]
    )


def trailing_two_kernel(
    s_ref, own_ref, cross_ref, c_ref, xs, xk, zs, zk, inv, inv2, rtab, ctab
):
    lo = s_ref[SLO]
    hi = s_ref[SHI]
    invert(s_ref, OWN, NC, inv, 18)
    invert(s_ref, MAP2, NU, inv2, 18)
    m, x, z, d = (
        NP + 3 * (2 * a + b) for a, b in ((hi, lo), (1 - hi, lo), (hi, 1 - lo), (1 - hi, 1 - lo))
    )
    for out_ref, tiles in (
        (xs, chain_x(x, m, d, z)),
        (xk, chain_x(m, x, z, d)),
        (zs, chain_z(z, d, m, x)),
        (zk, chain_z(m, x, z, d)),
    ):
        for n, (rq, cq, (r, c)) in enumerate(tiles):
            rtab[n] = rq + r
            ctab[n] = cq + c

        def tile(t, _):
            source_tile(lo, inv, inv2, own_ref, cross_ref, c_ref, out_ref, t, rtab[t], ctab[t])
            return 0

        lax.fori_loop(0, len(tiles), tile, 0)


def panel_two_kernel(
    s_ref, r_ref, xk, x1, x2, zk, z1, z2, lh, ll, wh, wl, p_ref, ph, plo, gh, gl
):
    for r in range(3):
        for c in range(3):
            t = 3 * r + c
            dst = (slice(r * T, r * T + T), slice(c * T, c * T + T))
            fill = s_ref[FILL2 + 6 * r + c].astype(f32)
            p_ref[dst] = r_ref[dst] * fill + ((xk[9 + t] + x1[9 + t]) + x2[t])
            dst = (dst[0], slice((c + 3) * T, (c + 4) * T))
            fill = s_ref[FILL2 + 6 * r + c + 3].astype(f32)
            p_ref[dst] = r_ref[dst] * fill + ((zk[9 + t] + z1[9 + t]) + z2[t])
    solve(p_ref, s_ref[LIVE2], lh, ll, wh, wl, ph, plo, gh, gl)


def schur_base_kernel(s_ref, r_ref, p_ref, xk, x1, x2, zk, z1, z2, out_ref):
    hi = s_ref[SHI]
    lo = s_ref[SLO]
    out_ref[...] = r_ref[:, NP * T :]
    m, x, z, d = (
        3 * (2 * a + b) for a, b in ((hi, lo), (1 - hi, lo), (hi, 1 - lo), (1 - hi, 1 - lo))
    )
    mine = split(p_ref[...])
    cols = pl.ds(pl.multiple_of(m * T, T), 384)
    out_ref[:, cols] = out_ref[:, cols] - dot3(mine, mine, NT)

    def add(quarter, r, c, value):
        out_ref[r * T : r * T + T, tl(quarter + c)] += value

    for k, r1, r2, diag, cross, pair in ((xk, x1, x2, DX, GX, z), (zk, z1, z2, DZ, GZ, x)):
        nd = len(diag)
        ng = len(cross)
        base = nd + ng + 9
        for n, (r, c) in enumerate(diag):
            v = (k[base + n] + r1[base + n]) + r2[n]
            add(m, r, c, v)
            if r != c:
                add(m, c, r, v.T)
        for n, (r, c) in enumerate(cross):
            v = (k[base + nd + n] + r1[base + nd + n]) + r2[nd + n]
            add(d, r, c, v)
        for n, (r, c) in enumerate(NINE):
            v = (k[nd + ng + n] + r1[nd + ng + n]) + r2[nd + ng + 3 * c + r].T
            add(pair, r, c, v)


def schur_near_kernel(s_ref, b_ref, p_ref, px, pz, out_ref):
    hi = s_ref[SHI]
    lo = s_ref[SLO]
    mine = split(p_ref[...])
    out_ref[...] = b_ref[...]
    for a, b, other in ((1 - hi, lo, px), (hi, 1 - lo, pz)):
        cols = pl.ds(pl.multiple_of((2 * a + b) * 384, T), 384)
        out_ref[:, cols] = b_ref[:, cols] - dot3(mine, split(other[...]), NT)


def schur_far_kernel(s_ref, b_ref, p_ref, pd0, pd1, out_ref):
    other = split(jnp.concatenate([pd0[...], pd1[...]], axis=0))
    out_ref[...] = b_ref[...] - dot3(split(p_ref[...]), other, NT)


def across(axis, values):
    size = lax.axis_size(axis)
    return lax.ppermute(values, axis, [(i, i ^ (size // 2)) for i in range(size)])


def program(
    contribution,
    pivot_one,
    rows_one,
    pivot_two,
    rows_two_in,
    map_one,
    map_two,
    fill_one,
    fill_two,
    live_one,
    live_two,
):
    size_lo = lax.axis_size("lo")
    size_hi = lax.axis_size("hi")
    half_lo = size_lo // 2
    half_hi = size_hi // 2
    lo = lax.axis_index("lo")
    hi = lax.axis_index("hi")
    side_lo = lo // half_lo
    side_hi = hi // half_hi
    front_lo = lo % half_lo
    front_hi = hi % half_hi
    quarter = 2 * side_hi + side_lo
    i32 = jnp.int32
    c = contribution[0, 0]
    rows1 = rows_one[0, 0]
    rows2 = rows_two_in[0, 0]
    smem = pltpu.SMEM((18,), i32)
    n = NP * T

    own_map = map_one[hi, lo]
    (piv_a,) = call(
        functools.partial(gather_a_kernel, half_lo),
        [own_map, c, pivot_one[0, 0]],
        [None, block(384, 256, 0)],
        [shape(11, T, T)],
        [smem],
    )
    piv_a, map_one, map_two, fill_one, fill_two, live_one, live_two, own_map = (
        lax.optimization_barrier(
            (piv_a, map_one, map_two, fill_one, fill_two, live_one, live_two, own_map)
        )
    )
    got_a = across("lo", piv_a)
    piv_b, coup = call(
        functools.partial(gather_b_kernel, half_lo),
        [own_map, c, pivot_one[0, 0]],
        [None, None],
        [shape(10, T, T), shape(16, T, T)],
        [smem],
    )
    scalars = jnp.concatenate(
        [
            map_one[hi, lo],
            map_one[hi, (lo + half_lo) % size_lo],
            map_two[hi, front_lo],
            jnp.stack([side_lo, side_hi]).astype(i32),
            live_one[hi, front_lo][None],
            live_two[front_hi, front_lo][None],
            lax.dynamic_slice_in_dim(fill_one[hi, front_lo], side_lo * 6, 6, 0).reshape(36),
            lax.dynamic_slice_in_dim(fill_two[front_hi, front_lo], quarter * 3, 3, 0).reshape(18),
        ]
    )
    piv_b, got_a = lax.optimization_barrier((piv_b, got_a))
    got_b = across("lo", piv_b)
    part = factor(scalars, [(piv_a, got_a)], BY_COL, 0, 2, (), LIVE1, None, n)
    later, *part = lax.optimization_barrier((scalars, *part))
    (x_one,) = call(
        couple_one_kernel,
        [later, rows1, c],
        [block(n, n, 0), None],
        [shape(n, n)],
        [smem],
    )
    coup, got_b = lax.optimization_barrier((coup, got_b))
    coup_got = across("lo", coup)
    lower_one, *fac1 = factor(
        scalars,
        [(piv_b, got_b)],
        BY_COL[11:],
        2,
        NP,
        part,
        LIVE1,
        lambda s: s[SLO] * 384,
        384,
    )
    panel_one, send = call(
        panel_one_kernel,
        [scalars, x_one, coup_got, *fac1],
        [None] * 6,
        [shape(n, n), shape(n, n // 2)],
        [pltpu.VMEM((n, n), bf16)] * 2 + [pltpu.VMEM((n, 2 * T), bf16)] * 2 + [smem],
        flops=3_000_000_000,
    )
    got = across("lo", send)
    own, piv = call(
        own_kernel,
        [scalars, panel_one, rows1, rows1, c, pivot_two[0, 0]],
        [None, block(n, n, 1), block(n, n, 2), None, None],
        [shape(n, n), shape(21, T, T)],
        [pltpu.VMEM((n, n), bf16)] * 2 + [pltpu.VMEM((2 * T, n), f32), smem, smem],
        flops=4_000_000_000,
    )
    half_cols = pl.BlockSpec((n, n // 2), lambda i, s: (0, s[SLO]))
    pa, pb = call(
        cross_pivot_kernel,
        [scalars, panel_one, got, piv],
        [half_cols, None, None],
        [shape(10, T, T), shape(11, T, T)],
        [smem],
        flops=500_000_000,
    )
    pa1 = across("hi", pa)
    pb1 = across("lo", pb)
    pa, pb, got = lax.optimization_barrier((pa, pb, got))
    (cross,) = call(
        cross_kernel,
        [scalars, panel_one, got, rows1],
        [half_cols, None, block(n, n, 2)],
        [shape(n, n)],
        [],
        flops=2_000_000_000,
    )
    cxs, cxk, czs, czk = rows_two(scalars, own, cross, c, 0, NP)
    pa = pa + pa1
    pb = pb + pb1
    pa2 = across("lo", pa)
    pb2 = across("hi", pb)
    cx1 = across("hi", cxs)
    cz1 = across("lo", czs)
    txs, txk, tzs, tzk = call(
        trailing_two_kernel,
        [scalars, own, cross, c],
        [None] * 3,
        [shape(23, T, T)] * 2 + [shape(25, T, T)] * 2,
        [smem, smem] + [pltpu.SMEM((32,), i32)] * 2,
    )
    tx1 = across("hi", txs)
    tz1 = across("lo", tzs)
    lower_two, *fac2 = factor(
        scalars,
        [(pa, pa2), (pb, pb2)],
        BY_ROW,
        0,
        NP,
        (),
        LIVE2,
        lambda s: (2 * s[SHI] + s[SLO]) * 192,
        192,
    )
    cx2 = across("lo", cxk[:9] + cx1[:9])
    cz2 = across("hi", czk[:9] + cz1[:9])
    tx = txk[:16] + tx1[:16]
    tz = tzk[:17] + tz1[:17]
    tx2 = across("lo", tx)
    tz2 = across("hi", tz)
    (panel_two,) = call(
        panel_two_kernel,
        [scalars, rows2, cxk, cx1, cx2, czk, cz1, cz2, *fac2],
        [block(384, n, 0)] + [None] * 10,
        [shape(384, n)],
        [pltpu.VMEM((384, n), bf16)] * 2 + [pltpu.VMEM((n, 2 * T), bf16)] * 2,
        flops=2_000_000_000,
    )
    px = across("hi", panel_two)
    pz = across("lo", panel_two)
    pd0 = across("hi", pz[:192])
    pd1 = across("lo", px[192:])
    (base_two,) = call(
        schur_base_kernel,
        [scalars, rows2, panel_two, txk, tx1, tx2, tzk, tz1, tz2],
        [None] * 8,
        [shape(384, NU * T)],
        [],
        flops=1_000_000_000,
    )
    (near_two,) = call(
        schur_near_kernel,
        [scalars, base_two, panel_two, px, pz],
        [None] * 4,
        [shape(384, NU * T)],
        [],
        flops=2_000_000_000,
    )
    far = pl.BlockSpec((384, 384), lambda i, s: (0, 2 * (1 - s[SHI]) + 1 - s[SLO]))
    (schur_two,) = call(
        schur_far_kernel,
        [scalars, near_two, panel_two, pd0, pd1],
        [far, None, None, None],
        [shape(384, NU * T)],
        [],
        flops=1_000_000_000,
        out_specs=[far],
        aliases={1: 0},
    )
    return tuple(
        out[None, None] for out in (lower_one, panel_one, lower_two, panel_two, schur_two)
    )


def solution(mesh):
    split_spec = P("hi", "lo", None, None)
    return jax.shard_map(
        program,
        mesh=mesh,
        in_specs=(split_spec,) * 5 + (P(),) * 6,
        out_specs=(split_spec,) * 5,
        check_vma=False,
    )
```
